32 devices in a mesh: particle: 2 (over x), coil: 8 (over z, y), phase: 2 (over core).
Axes of the slice: x: 2, y: 2, z: 4, core: 2. Of those that a mesh axis runs over, the one named last changes fastest.
Arguments:
- position: float32 [256, 16, 4, 384], P('coil', 'phase', 'particle'), parts along dimension 2, may hold values from -6 to 6
- coil_maps: bfloat16 [8, 256, 4, 384], P('coil', None, 'particle'), parts along dimension 2, may hold values from -2 to 2
- kspace_data: bfloat16 [8, 256, 16, 4, 384], P('coil', None, 'phase', 'particle'), parts along dimension 3, may hold values from -1.796875 to 1.796875
- sample_mask: int32 [256, 16], P(None, 'phase'), may hold values 0 or 1
Outputs:
- gradient: float32 [256, 16, 4, 384], P('coil', 'phase', 'particle'), parts along dimension 2
The draws below stay inside these ranges and needn't reach their ends.
There are 2 independent parts, one for each index of `particle`. The reference program is written for one: setup_inputs(seed, part) draws one part's arguments, and reference() takes and returns one part's arrays. A program takes and returns all parts, laid end to end along the dimension named above; an argument that names none is the same for every part. Nothing has to cross between parts.
All inputs are finite; a program needn't handle non-finite values. No bound on the sum of `sample_mask` on one device may be relied on, other than what follows from the above.
Results may differ from the reference program's by a relative error of at most 0.0012.
Values may be sent and summed in bfloat16 or wider, within the bound.
A program may use at most 64 MiB of HBM per device.

```python
import math
import jax
import jax.numpy as jnp
from jax import lax

NA = 256
NB = 192
SLICES = 2
PHASES = 16
COILS = 8


def set_ends(result, key, least, top_value):
    longest = result.shape.index(max(result.shape))
    spots = []
    for shift in (0, 1):
        where = [jax.random.randint(jax.random.fold_in(key, axis), (), 0, length) for axis, length in enumerate(result.shape)]
        where[longest] = (where[longest] + shift) % result.shape[longest]
        spots.append(tuple(where))
    return result.at[spots[0]].set(least).at[spots[1]].set(top_value)


def steps_of(own_key, extent, shards, low, top_value):
    factor_of = 1.0
    for dim, shards_of in shards:
        draws = jax.random.uniform(jax.random.fold_in(jax.random.fold_in(own_key, 6), dim), (shards_of,), jnp.float32, low / len(shards), top_value / len(shards))
        factor_of = factor_of * jnp.repeat(jnp.exp(draws), extent[dim] // shards_of).reshape((-1,) + (1,) * (len(extent) - 1 - dim))
    return factor_of


def scatter_about(stream_key, extent, scale, limit, cuts=(), kind=jnp.bfloat16):
    loudness = steps_of(stream_key, extent, cuts, -0.22, 0.18) if cuts else 1.0
    drawn = jax.random.normal(stream_key, extent, jnp.float32) * scale * loudness
    return jnp.minimum(jnp.maximum(drawn, -limit), limit).astype(kind)


def setup_inputs(seed: int = 0, part: int = 0) -> dict:
    streams_of = jax.random.split(jax.random.key(seed), 5)
    own_keys = jax.random.split(jax.random.fold_in(streams_of[4], part), 5)
    position = scatter_about(own_keys[0], (NA, PHASES, SLICES, 2 * NB), 1.0, 6.0, ((0, 8), (1, 2)), jnp.float32)
    coil_maps = scatter_about(own_keys[1], (COILS, NA, SLICES, 2 * NB), COILS ** -0.5, 2.0, ((0, 8),))
    kspace_data = scatter_about(own_keys[2], (COILS, NA, PHASES, SLICES, 2 * NB), 0.3, 1.796875, ((0, 8), (2, 2)))
    sample_mask = set_ends((jax.random.randint(streams_of[3], (NA, PHASES), 0, 3) < 1).astype(jnp.int32), jax.random.fold_in(streams_of[3], 1), 0, 1)
    return dict(position=position, coil_maps=coil_maps, kspace_data=kspace_data, sample_mask=sample_mask)


def dft_tables(length):
    counter = jnp.arange(length, dtype=jnp.int32)
    product = counter[:, None] * counter[None, :] % length
    angles = product.astype(jnp.float32) * (2.0 * math.pi / length)
    scaling = 1.0 / math.sqrt(length)
    return (jnp.cos(angles) * scaling, -jnp.sin(angles) * scaling)

def build_tables(rows_total, width):
    row_real, row_imag = dft_tables(rows_total)
    col_real, col_imag = dft_tables(width)
    forward_wide = jnp.concatenate([jnp.concatenate([col_real, col_imag], 1), jnp.concatenate([-col_imag, col_real], 1)], 0)
    backward_wide = jnp.concatenate([jnp.concatenate([col_real, -col_imag], 1), jnp.concatenate([col_imag, col_real], 1)], 0)
    return (row_real.astype(jnp.bfloat16), row_imag.astype(jnp.bfloat16), forward_wide.astype(jnp.bfloat16), backward_wide.astype(jnp.bfloat16))

def complex_times(factor, values, conjugate):
    width = values.shape[-1] // 2
    factor_real = factor[..., :width]
    factor_imag = factor[..., width:]
    if conjugate:
        factor_imag = -factor_imag
    value_real = values[..., :width]
    value_imag = values[..., width:]
    out_real = factor_real * value_real - factor_imag * value_imag
    out_imag = factor_real * value_imag + factor_imag * value_real
    return jnp.concatenate([out_real, out_imag], -1)

def rows_apply(table_real, table_imag, values, adjoint):
    width = values.shape[-1] // 2
    real_part = jnp.einsum('kn,npsd->kpsd', table_real.astype(jnp.float32), values.astype(jnp.float32))
    imag_part = jnp.einsum('kn,npsd->kpsd', table_imag.astype(jnp.float32), values.astype(jnp.float32))
    if adjoint:
        out_real = real_part[..., :width] + imag_part[..., width:]
        out_imag = real_part[..., width:] - imag_part[..., :width]
    else:
        out_real = real_part[..., :width] - imag_part[..., width:]
        out_imag = real_part[..., width:] + imag_part[..., :width]
    return jnp.concatenate([out_real, out_imag], -1)

def reference(position, coil_maps, kspace_data, sample_mask):
    rows_total = position.shape[0]
    width = position.shape[3] // 2
    row_real, row_imag, forward_wide, backward_wide = build_tables(rows_total, width)
    position_low = position.astype(jnp.bfloat16)
    sample_weight = sample_mask.astype(jnp.float32)[:, :, None, None]

    def per_coil(total, inputs):
        coil_map, coil_data = inputs
        map_wide = coil_map.astype(jnp.float32)[:, None]
        lifted = complex_times(map_wide, position_low.astype(jnp.float32), False).astype(jnp.bfloat16)
        spread = jnp.einsum('npsc,cd->npsd', lifted.astype(jnp.float32), forward_wide.astype(jnp.float32)).astype(jnp.bfloat16)
        kspace = rows_apply(row_real, row_imag, spread, False)
        residual = (sample_weight * (kspace - coil_data.astype(jnp.float32))).astype(jnp.bfloat16)
        back_rows = rows_apply(row_real, row_imag, residual, True).astype(jnp.bfloat16)
        back = jnp.einsum('npsc,cd->npsd', back_rows.astype(jnp.float32), backward_wide.astype(jnp.float32))
        return (total + complex_times(map_wide, back, True), None)
    zeros = jnp.zeros(position.shape, jnp.float32)
    likelihood, unused = lax.scan(per_coil, zeros, (coil_maps, kspace_data))
    phase_part = 2.0 * position - jnp.roll(position, 1, axis=1) - jnp.roll(position, -1, axis=1)
    row_part = 2.0 * position - jnp.roll(position, 1, axis=0) - jnp.roll(position, -1, axis=0)
    return 0.6 * likelihood + 0.5 * phase_part + 0.3 * row_part
```

```python
import functools
import math

import jax
import jax.numpy as jnp
import ml_dtypes
import numpy as np
from jax import lax
from jax.experimental import pallas as pl
from jax.experimental.pallas import tpu as pltpu
from jax.sharding import PartitionSpec as P

MESH = pl.DeviceIdType.MESH
YS = 2


def dft_tables(length):
    counter = np.arange(length, dtype=np.int32)
    product = counter[:, None] * counter[None, :] % length
    angles = product.astype(np.float32) * np.float32(2.0 * math.pi / length)
    scaling = np.float32(1.0 / math.sqrt(length))
    return (np.cos(angles) * scaling, -np.sin(angles) * scaling)


def wide_tables(width):
    col_real, col_imag = dft_tables(width)
    forward = np.block([[col_real, col_imag], [-col_imag, col_real]])
    backward = np.block([[col_real, -col_imag], [col_imag, col_real]])
    return forward.astype(ml_dtypes.bfloat16), backward.astype(ml_dtypes.bfloat16)


def row_tables(rows_total):
    row_real, row_imag = dft_tables(rows_total)
    return row_real.astype(ml_dtypes.bfloat16), row_imag.astype(ml_dtypes.bfloat16)


def kernel(
    zs, phases, rows, width,
    pos_ref, edge_ref, map_ref, data_ref, mask_ref, rf_ref, rb_ref, wf_ref, wb_ref,
    out_ref,
    low, gath, posx, halo_rows, fac_a, fac_b, vv, rr, ysend, yrecv, pown, own, zsend, zrecv,
    agz_s, agz_r, agy_s, agy_r, rsy_s, rsy_r, rsz_s, rsz_r, ph_s, ph_r, hr_s, hr_r,
):
    half = width // 2
    lanes = pos_ref.shape[2]
    slices = lanes // width
    side = zs * rows
    total = YS * side
    coils = zs * YS
    coil = lax.axis_index("coil")
    z = coil // YS
    y = coil % YS
    other_y = 1 - y
    partner = z * YS + other_y
    phase_count = lax.axis_size("phase")
    ph = lax.axis_index("phase")
    ph_next = lax.rem(ph + 1, phase_count)
    ph_prev = lax.rem(ph + phase_count - 1, phase_count)
    c_next = lax.rem(coil + 1, coils)
    c_prev = lax.rem(coil + coils - 1, coils)
    z_to = [lax.rem(z + j, zs) for j in range(1, zs)]

    barrier = pltpu.get_barrier_semaphore()
    peers = [{"coil": t * YS + y} for t in z_to] + [{"coil": partner}]
    peers += [{"coil": c_next}, {"coil": c_prev}, {"phase": ph_next}, {"phase": ph_prev}]
    for peer in peers:
        pl.semaphore_signal(barrier, inc=1, device_id=peer, device_id_type=MESH)

    @pl.loop(0, phases)
    def _(p):
        low[p] = pos_ref[p].astype(jnp.bfloat16)

    @pl.loop(0, phases)
    def _(p):
        gath[p, y, z] = low[p]
        posx[p + 1] = pos_ref[p]

    pl.semaphore_wait(barrier, len(peers))

    def ag_z(p, j):
        return pltpu.make_async_remote_copy(
            src_ref=low.at[p], dst_ref=gath.at[p, y, z],
            send_sem=agz_s.at[p, j], recv_sem=agz_r.at[p, j],
            device_id={"coil": z_to[j] * YS + y}, device_id_type=MESH,
        )

    def ag_y(p):
        return pltpu.make_async_remote_copy(
            src_ref=gath.at[p, y], dst_ref=gath.at[p, y],
            send_sem=agy_s.at[p], recv_sem=agy_r.at[p],
            device_id={"coil": partner}, device_id_type=MESH,
        )

    def rs_y(p):
        return pltpu.make_async_remote_copy(
            src_ref=ysend.at[p], dst_ref=yrecv.at[p],
            send_sem=rsy_s.at[p], recv_sem=rsy_r.at[p],
            device_id={"coil": partner}, device_id_type=MESH,
        )

    def rs_z(p, j):
        return pltpu.make_async_remote_copy(
            src_ref=zsend.at[p, z_to[j]], dst_ref=zrecv.at[p, j],
            send_sem=rsz_s.at[p, j], recv_sem=rsz_r.at[p, j],
            device_id={"coil": z_to[j] * YS + y}, device_id_type=MESH,
        )

    def halo_copies():
        yield pltpu.make_async_remote_copy(
            src_ref=pos_ref.at[phases - 1], dst_ref=posx.at[0],
            send_sem=ph_s.at[0], recv_sem=ph_r.at[0],
            device_id={"phase": ph_next}, device_id_type=MESH,
        )
        yield pltpu.make_async_remote_copy(
            src_ref=pos_ref.at[0], dst_ref=posx.at[phases + 1],
            send_sem=ph_s.at[1], recv_sem=ph_r.at[1],
            device_id={"phase": ph_prev}, device_id_type=MESH,
        )
        yield pltpu.make_async_remote_copy(
            src_ref=edge_ref.at[1], dst_ref=halo_rows.at[0],
            send_sem=hr_s.at[0], recv_sem=hr_r.at[0],
            device_id={"coil": c_next}, device_id_type=MESH,
        )
        yield pltpu.make_async_remote_copy(
            src_ref=edge_ref.at[0], dst_ref=halo_rows.at[1],
            send_sem=hr_s.at[1], recv_sem=hr_r.at[1],
            device_id={"coil": c_prev}, device_id_type=MESH,
        )

    @pl.loop(0, phases)
    def _(p):
        for j in range(zs - 1):
            ag_z(p, j).start()

    for copy in halo_copies():
        copy.start()

    first = lax.broadcasted_iota(jnp.int32, (total, width), 1) < half
    for s in range(slices):
        cols = slice(s * width, (s + 1) * width)
        plain = map_ref[:, cols].astype(jnp.float32)
        turned = pltpu.roll(plain, half, 1)
        fac_a[:, cols] = jnp.where(first, plain, turned)
        fac_b[:, cols] = jnp.where(first, -turned, plain)

    def forward(p):
        for j in range(zs - 1):
            ag_z(p, j).wait_recv()
        ag_y(p).start()

    def compute(p):
        for s in range(slices):
            cols = slice(s * width, (s + 1) * width)
            x = gath[p, :, :, :, cols].reshape(total, width).astype(jnp.float32)
            lifted = fac_a[:, cols] * x + fac_b[:, cols] * pltpu.roll(x, half, 1)
            spread = jnp.dot(
                lifted.astype(jnp.bfloat16), wf_ref[...], preferred_element_type=jnp.float32
            ).astype(jnp.bfloat16)
            vv[:total, cols] = spread[:, :width]
            vv[total:, cols] = spread[:, width:]
        weight = mask_ref[p]
        for s in range(slices):
            cols = slice(s * width, (s + 1) * width)
            kspace = jnp.dot(rf_ref[...], vv[:, cols], preferred_element_type=jnp.float32)
            residual = weight * (kspace - data_ref[p, :, cols].astype(jnp.float32))
            turned = pltpu.roll(residual, half, 1)
            rr[:total, cols] = residual.astype(jnp.bfloat16)
            rr[total:, cols] = jnp.where(first, turned, -turned).astype(jnp.bfloat16)
        for s in range(slices):
            cols = slice(s * width, (s + 1) * width)
            back_rows = jnp.dot(
                rb_ref[...], rr[:, cols], preferred_element_type=jnp.float32
            ).astype(jnp.bfloat16)
            back = jnp.dot(back_rows, wb_ref[...], preferred_element_type=jnp.float32)
            pown[p, :, :, cols] = (
                fac_a[:, cols] * back[:, :width] - fac_b[:, cols] * back[:, width:]
            ).reshape(YS, side, width)
        ysend[p] = pown[p, other_y].astype(jnp.bfloat16)

    def middle(p):
        rs_y(p).wait_recv()
        summed = pown[p, y] + yrecv[p].astype(jnp.float32)
        pown[p, y] = summed
        zsend[p] = summed.astype(jnp.bfloat16).reshape(zs, rows, lanes)
        for j in range(zs - 1):
            rs_z(p, j).start()
        own[p] = pown[p, y, pl.ds(pl.multiple_of(z * rows, rows), rows), :]

    forward(0)

    @pl.loop(0, phases)
    def _(p):
        @pl.when(p + 1 < phases)
        def _():
            forward(p + 1)

        ag_y(p).wait_recv()
        compute(p)
        rs_y(p).start()

        @pl.when(p >= 1)
        def _():
            middle(p - 1)

    middle(phases - 1)

    for copy in halo_copies():
        copy.wait()

    row = lax.broadcasted_iota(jnp.int32, (rows, lanes), 0)

    @pl.loop(0, phases)
    def _(p):
        for j in range(zs - 1):
            rs_z(p, j).wait_recv()
        likelihood = own[p]
        for j in range(zs - 1):
            likelihood = likelihood + zrecv[p, j].astype(jnp.float32)
        here = posx[p + 1]
        phase_part = 2.0 * here - posx[p] - posx[p + 2]
        above = jnp.where(row == 0, halo_rows[0, p], pltpu.roll(here, 1, 0))
        below = jnp.where(row == rows - 1, halo_rows[1, p], pltpu.roll(here, rows - 1, 0))
        row_part = 2.0 * here - above - below
        out_ref[p] = 0.6 * likelihood + 0.5 * phase_part + 0.3 * row_part

    @pl.loop(0, phases)
    def _(p):
        for j in range(zs - 1):
            ag_z(p, j).wait_send()
            rs_z(p, j).wait_send()
        ag_y(p).wait_send()
        rs_y(p).wait_send()


def fused(position, coil_maps, kspace_data, sample_mask):
    rows, phases, slices, width = position.shape
    total = coil_maps.shape[1]
    zs = total // rows // YS
    side = zs * rows
    lanes = slices * width
    order = np.arange(total).reshape(zs, YS, rows).transpose(1, 0, 2).reshape(-1)
    row_real, row_imag = row_tables(total)
    rf = np.concatenate([row_real[:, order], row_imag[:, order]], 1)
    rb = np.concatenate([row_real[order], row_imag[order]], 1)
    forward, backward = wide_tables(width // 2)
    half = width // 2
    wf = np.concatenate([forward, -forward[:, half:], forward[:, :half]], 1)
    wb = np.concatenate([backward, backward[:, half:], backward[:, :half]], 1)

    pos = position.transpose(1, 0, 2, 3).reshape(phases, rows, lanes)
    edges = jnp.stack([position[0], position[-1]]).reshape(2, phases, 1, lanes)
    maps = coil_maps[0].reshape(zs, YS, rows, lanes).transpose(1, 0, 2, 3).reshape(total, lanes)
    data = kspace_data[0].transpose(1, 0, 2, 3).reshape(phases, total, lanes)
    weight = sample_mask.astype(jnp.float32).T[:, :, None]

    vmem = pltpu.VMEM
    bf16, f32 = jnp.bfloat16, jnp.float32
    dma = pltpu.SemaphoreType.DMA
    result = pl.pallas_call(
        functools.partial(kernel, zs, phases, rows, width),
        out_shape=jax.ShapeDtypeStruct((phases, rows, lanes), f32),
        in_specs=[pl.BlockSpec(memory_space=vmem)] * 9,
        out_specs=pl.BlockSpec(memory_space=vmem),
        scratch_shapes=[
            vmem((phases, rows, lanes), bf16),
            vmem((phases, YS, zs, rows, lanes), bf16),
            vmem((phases + 2, rows, lanes), f32),
            vmem((2, phases, 1, lanes), f32),
            vmem((total, lanes), f32),
            vmem((total, lanes), f32),
            vmem((2 * total, lanes), bf16),
            vmem((2 * total, lanes), bf16),
            vmem((phases, side, lanes), bf16),
            vmem((phases, side, lanes), bf16),
            vmem((phases, YS, side, lanes), f32),
            vmem((phases, rows, lanes), f32),
            vmem((phases, zs, rows, lanes), bf16),
            vmem((phases, zs - 1, rows, lanes), bf16),
            dma((phases, zs - 1)), dma((phases, zs - 1)),
            dma((phases,)), dma((phases,)),
            dma((phases,)), dma((phases,)),
            dma((phases, zs - 1)), dma((phases, zs - 1)),
            dma((2,)), dma((2,)), dma((2,)), dma((2,)),
        ],
        compiler_params=pltpu.CompilerParams(
            collective_id=0, has_side_effects=True, vmem_limit_bytes=56 << 20
        ),
    )(pos, edges, maps, data, weight, jnp.asarray(rf), jnp.asarray(rb), jnp.asarray(wf), jnp.asarray(wb))
    return result.reshape(phases, rows, slices, width).transpose(1, 0, 2, 3)


def with_halo(block, sides, width):
    for axis, dim in sides:
        count = lax.axis_size(axis)
        forward = [(i, i + 1) for i in range(count - 1)]
        forward.append((count - 1, 0))
        backward = [(target, source) for source, target in forward]
        low = lax.ppermute(
            lax.slice_in_dim(block, block.shape[dim] - width, None, axis=dim), axis, forward
        )
        high = lax.ppermute(lax.slice_in_dim(block, 0, width, axis=dim), axis, backward)
        block = jnp.concatenate([low, block, high], axis=dim)
    return block


def complex_times(factor, values, conjugate):
    width = values.shape[-1] // 2
    factor_real = factor[..., :width]
    factor_imag = factor[..., width:]
    if conjugate:
        factor_imag = -factor_imag
    value_real = values[..., :width]
    value_imag = values[..., width:]
    out_real = factor_real * value_real - factor_imag * value_imag
    out_imag = factor_real * value_imag + factor_imag * value_real
    return jnp.concatenate([out_real, out_imag], -1)


def rows_apply(table_real, table_imag, values, adjoint):
    width = values.shape[-1] // 2
    real_part = jnp.einsum("kn,npsd->kpsd", table_real, values, preferred_element_type=jnp.float32)
    imag_part = jnp.einsum("kn,npsd->kpsd", table_imag, values, preferred_element_type=jnp.float32)
    if adjoint:
        out_real = real_part[..., :width] + imag_part[..., width:]
        out_imag = real_part[..., width:] - imag_part[..., :width]
    else:
        out_real = real_part[..., :width] - imag_part[..., width:]
        out_imag = real_part[..., width:] + imag_part[..., :width]
    return jnp.concatenate([out_real, out_imag], -1)


def general(position, coil_maps, kspace_data, sample_mask):
    rows_total = coil_maps.shape[1]
    width = position.shape[3] // 2
    row_real, row_imag = (jnp.asarray(t) for t in row_tables(rows_total))
    forward_wide, backward_wide = (jnp.asarray(t) for t in wide_tables(width))
    coil_data = kspace_data[0]
    sample_weight = sample_mask.astype(jnp.float32)[:, :, None, None]
    position_low = position.astype(jnp.bfloat16)
    map_rows = coil_maps[0].astype(jnp.float32)[:, None]
    image = lax.all_gather(position_low, "coil", axis=0, tiled=True)
    lifted = complex_times(map_rows, image.astype(jnp.float32), False).astype(jnp.bfloat16)
    spread = jnp.einsum(
        "npsc,cd->npsd", lifted, forward_wide, preferred_element_type=jnp.float32
    ).astype(jnp.bfloat16)
    kspace = rows_apply(row_real, row_imag, spread, False)
    residual = (sample_weight * (kspace - coil_data.astype(jnp.float32))).astype(jnp.bfloat16)
    back_rows = rows_apply(row_real, row_imag, residual, True).astype(jnp.bfloat16)
    back = jnp.einsum("npsc,cd->npsd", back_rows, backward_wide, preferred_element_type=jnp.float32)
    likelihood = lax.psum_scatter(
        complex_times(map_rows, back, True), "coil", scatter_dimension=0, tiled=True
    )
    padded = with_halo(position, (("coil", 0), ("phase", 1)), 1)
    phase_part = 2.0 * position - padded[1:-1, :-2] - padded[1:-1, 2:]
    row_part = 2.0 * position - padded[:-2, 1:-1] - padded[2:, 1:-1]
    return 0.6 * likelihood + 0.5 * phase_part + 0.3 * row_part


def local(position, coil_maps, kspace_data, sample_mask):
    rows = position.shape[0]
    coils = lax.axis_size("coil")
    if coils == 8 and rows % 16 == 0 and position.shape[3] % 128 == 0:
        return fused(position, coil_maps, kspace_data, sample_mask)
    return general(position, coil_maps, kspace_data, sample_mask)


def solution(mesh):
    in_specs = (
        P("coil", "phase", "particle", None),
        P("coil", None, "particle", None),
        P("coil", None, "phase", "particle", None),
        P(None, "phase"),
    )
    out_specs = P("coil", "phase", "particle", None)
    return jax.shard_map(local, mesh=mesh, in_specs=in_specs, out_specs=out_specs, check_vma=False)
```

```python
import functools
import math

import jax
import jax.numpy as jnp
import ml_dtypes
import numpy as np
from jax import lax
from jax.experimental import pallas as pl
from jax.experimental.pallas import tpu as pltpu
from jax.sharding import PartitionSpec as P

MESH = pl.DeviceIdType.MESH
YS = 2


def dft_tables(length):
    counter = np.arange(length, dtype=np.int32)
    product = counter[:, None] * counter[None, :] % length
    angles = product.astype(np.float32) * np.float32(2.0 * math.pi / length)
    scaling = np.float32(1.0 / math.sqrt(length))
    return (np.cos(angles) * scaling, -np.sin(angles) * scaling)


def wide_tables(width):
    col_real, col_imag = dft_tables(width)
    forward = np.block([[col_real, col_imag], [-col_imag, col_real]])
    backward = np.block([[col_real, -col_imag], [col_imag, col_real]])
    return forward.astype(ml_dtypes.bfloat16), backward.astype(ml_dtypes.bfloat16)


def row_tables(rows_total):
    row_real, row_imag = dft_tables(rows_total)
    return row_real.astype(ml_dtypes.bfloat16), row_imag.astype(ml_dtypes.bfloat16)


def kernel(
    zs, phases, rows, width,
    pos_ref, map_ref, data_hbm, mask_ref, rf_ref, rb_ref, wf_ref, wb_ref,
    out_ref,
    data, edge, mask, low, gath, posx, halo_rows, fac_a, fac_b, vv, rr, ysend, yrecv, pown, own, zsend, zrecv,
    agz_s, agz_r, agy_s, agy_r, rsy_s, rsy_r, rsz_s, rsz_r, ph_s, ph_r, hr_s, hr_r, data_s,
):
    half = width // 2
    slices = pos_ref.shape[2]
    lanes = slices * width
    side = zs * rows
    total = YS * side
    coils = zs * YS
    coil = lax.axis_index("coil")
    z = coil // YS
    y = coil % YS
    other_y = 1 - y
    partner = z * YS + other_y
    phase_count = lax.axis_size("phase")
    ph = lax.axis_index("phase")
    ph_next = lax.rem(ph + 1, phase_count)
    ph_prev = lax.rem(ph + phase_count - 1, phase_count)
    c_next = lax.rem(coil + 1, coils)
    c_prev = lax.rem(coil + coils - 1, coils)
    z_to = [lax.rem(z + j, zs) for j in range(1, zs)]

    barrier = pltpu.get_barrier_semaphore()
    peers = [{"coil": t * YS + y} for t in z_to] + [{"coil": partner}]
    peers += [{"coil": c_next}, {"coil": c_prev}, {"phase": ph_next}, {"phase": ph_prev}]
    for peer in peers:
        pl.semaphore_signal(barrier, inc=1, device_id=peer, device_id_type=MESH)

    def data_copy(p):
        return pltpu.make_async_copy(data_hbm.at[:, p], data.at[p], data_s.at[p])

    @pl.loop(0, phases)
    def _(p):
        data_copy(p).start()
        for s in range(slices):
            cols = slice(s * width, (s + 1) * width)
            posx[p + 1, :, cols] = pos_ref[:, p, s, :]
        here = posx[p + 1]
        edge[0, p] = here[:1]
        edge[1, p] = here[rows - 1:]
        low[p] = here.astype(jnp.bfloat16)
        gath[p, y, z] = low[p]

    pl.semaphore_wait(barrier, len(peers))

    def ag_z(p, j):
        return pltpu.make_async_remote_copy(
            src_ref=low.at[p], dst_ref=gath.at[p, y, z],
            send_sem=agz_s.at[p, j], recv_sem=agz_r.at[p, j],
            device_id={"coil": z_to[j] * YS + y}, device_id_type=MESH,
        )

    def ag_y(p):
        return pltpu.make_async_remote_copy(
            src_ref=gath.at[p, y], dst_ref=gath.at[p, y],
            send_sem=agy_s.at[p], recv_sem=agy_r.at[p],
            device_id={"coil": partner}, device_id_type=MESH,
        )

    def rs_y(p):
        return pltpu.make_async_remote_copy(
            src_ref=ysend.at[p], dst_ref=yrecv.at[p],
            send_sem=rsy_s.at[p], recv_sem=rsy_r.at[p],
            device_id={"coil": partner}, device_id_type=MESH,
        )

    def rs_z(p, j):
        return pltpu.make_async_remote_copy(
            src_ref=zsend.at[p, z_to[j]], dst_ref=zrecv.at[p, j],
            send_sem=rsz_s.at[p, j], recv_sem=rsz_r.at[p, j],
            device_id={"coil": z_to[j] * YS + y}, device_id_type=MESH,
        )

    def halo_copies():
        yield pltpu.make_async_remote_copy(
            src_ref=posx.at[phases], dst_ref=posx.at[0],
            send_sem=ph_s.at[0], recv_sem=ph_r.at[0],
            device_id={"phase": ph_next}, device_id_type=MESH,
        )
        yield pltpu.make_async_remote_copy(
            src_ref=posx.at[1], dst_ref=posx.at[phases + 1],
            send_sem=ph_s.at[1], recv_sem=ph_r.at[1],
            device_id={"phase": ph_prev}, device_id_type=MESH,
        )
        yield pltpu.make_async_remote_copy(
            src_ref=edge.at[1], dst_ref=halo_rows.at[0],
            send_sem=hr_s.at[0], recv_sem=hr_r.at[0],
            device_id={"coil": c_next}, device_id_type=MESH,
        )
        yield pltpu.make_async_remote_copy(
            src_ref=edge.at[0], dst_ref=halo_rows.at[1],
            send_sem=hr_s.at[1], recv_sem=hr_r.at[1],
            device_id={"coil": c_prev}, device_id_type=MESH,
        )

    @pl.loop(0, phases)
    def _(p):
        for j in range(zs - 1):
            ag_z(p, j).start()

    for copy in halo_copies():
        copy.start()

    first = lax.broadcasted_iota(jnp.int32, (total, width), 1) < half
    for s in range(slices):
        cols = slice(s * width, (s + 1) * width)
        plain = jnp.concatenate(
            [map_ref[pl.ds((b % zs * YS + b // zs) * rows, rows), cols] for b in range(coils)], 0
        ).astype(jnp.float32)
        turned = pltpu.roll(plain, half, 1)
        fac_a[:, cols] = jnp.where(first, plain, turned)
        fac_b[:, cols] = jnp.where(first, -turned, plain)

    mask[...] = mask_ref[...].astype(jnp.float32).T

    def forward(p):
        for j in range(zs - 1):
            ag_z(p, j).wait_recv()
        ag_y(p).start()

    def compute(p):
        for s in range(slices):
            cols = slice(s * width, (s + 1) * width)
            x = gath[p, :, :, :, cols].reshape(total, width).astype(jnp.float32)
            lifted = fac_a[:, cols] * x + fac_b[:, cols] * pltpu.roll(x, half, 1)
            spread = jnp.dot(
                lifted.astype(jnp.bfloat16), wf_ref[...], preferred_element_type=jnp.float32
            ).astype(jnp.bfloat16)
            vv[:total, cols] = spread[:, :width]
            vv[total:, cols] = spread[:, width:]
        lane = lax.broadcasted_iota(jnp.int32, mask.shape, 1)
        weight = jnp.sum(jnp.where(lane == p, mask[...], 0.0), axis=1, keepdims=True)
        data_copy(p).wait()
        for s in range(slices):
            cols = slice(s * width, (s + 1) * width)
            kspace = jnp.dot(rf_ref[...], vv[:, cols], preferred_element_type=jnp.float32)
            residual = weight * (kspace - data[p, :, s, :].astype(jnp.float32))
            turned = pltpu.roll(residual, half, 1)
            rr[:total, cols] = residual.astype(jnp.bfloat16)
            rr[total:, cols] = jnp.where(first, turned, -turned).astype(jnp.bfloat16)
        for s in range(slices):
            cols = slice(s * width, (s + 1) * width)
            back_rows = jnp.dot(
                rb_ref[...], rr[:, cols], preferred_element_type=jnp.float32
            ).astype(jnp.bfloat16)
            back = jnp.dot(back_rows, wb_ref[...], preferred_element_type=jnp.float32)
            pown[p, :, :, cols] = (
                fac_a[:, cols] * back[:, :width] - fac_b[:, cols] * back[:, width:]
            ).reshape(YS, side, width)
        ysend[p] = pown[p, other_y].astype(jnp.bfloat16)

    def middle(p):
        rs_y(p).wait_recv()
        summed = pown[p, y] + yrecv[p].astype(jnp.float32)
        pown[p, y] = summed
        zsend[p] = summed.astype(jnp.bfloat16).reshape(zs, rows, lanes)
        for j in range(zs - 1):
            rs_z(p, j).start()
        own[p] = pown[p, y, pl.ds(pl.multiple_of(z * rows, rows), rows), :]

    forward(0)

    @pl.loop(0, phases)
    def _(p):
        @pl.when(p + 1 < phases)
        def _():
            forward(p + 1)

        ag_y(p).wait_recv()
        compute(p)
        rs_y(p).start()

        @pl.when(p >= 1)
        def _():
            middle(p - 1)

    middle(phases - 1)

    for copy in halo_copies():
        copy.wait()

    row = lax.broadcasted_iota(jnp.int32, (rows, lanes), 0)

    @pl.loop(0, phases)
    def _(p):
        for j in range(zs - 1):
            rs_z(p, j).wait_recv()
        likelihood = own[p]
        for j in range(zs - 1):
            likelihood = likelihood + zrecv[p, j].astype(jnp.float32)
        here = posx[p + 1]
        phase_part = 2.0 * here - posx[p] - posx[p + 2]
        above = jnp.where(row == 0, halo_rows[0, p], pltpu.roll(here, 1, 0))
        below = jnp.where(row == rows - 1, halo_rows[1, p], pltpu.roll(here, rows - 1, 0))
        row_part = 2.0 * here - above - below
        grad = 0.6 * likelihood + 0.5 * phase_part + 0.3 * row_part
        for s in range(slices):
            out_ref[:, p, s, :] = grad[:, s * width : (s + 1) * width]

    @pl.loop(0, phases)
    def _(p):
        for j in range(zs - 1):
            ag_z(p, j).wait_send()
            rs_z(p, j).wait_send()
        ag_y(p).wait_send()
        rs_y(p).wait_send()


def fused(position, coil_maps, kspace_data, sample_mask):
    rows, phases, slices, width = position.shape
    total = coil_maps.shape[1]
    zs = total // rows // YS
    side = zs * rows
    lanes = slices * width
    order = np.arange(total).reshape(zs, YS, rows).transpose(1, 0, 2).reshape(-1)
    row_real, row_imag = row_tables(total)
    rf = np.concatenate([row_real[:, order], row_imag[:, order]], 1)
    rb = np.concatenate([row_real[order], row_imag[order]], 1)
    forward, backward = wide_tables(width // 2)
    half = width // 2
    wf = np.concatenate([forward, -forward[:, half:], forward[:, :half]], 1)
    wb = np.concatenate([backward, backward[:, half:], backward[:, :half]], 1)

    maps = coil_maps[0].reshape(total, lanes)

    vmem = pltpu.VMEM
    bf16, f32 = jnp.bfloat16, jnp.float32
    dma = pltpu.SemaphoreType.DMA
    return pl.pallas_call(
        functools.partial(kernel, zs, phases, rows, width),
        out_shape=jax.ShapeDtypeStruct(position.shape, f32),
        in_specs=[pl.BlockSpec(memory_space=pl.ANY if i == 2 else vmem) for i in range(8)],
        out_specs=pl.BlockSpec(memory_space=vmem),
        scratch_shapes=[
            vmem((phases, total, slices, width), bf16),
            vmem((2, phases, 1, lanes), f32),
            vmem((total, phases), f32),
            vmem((phases, rows, lanes), bf16),
            vmem((phases, YS, zs, rows, lanes), bf16),
            vmem((phases + 2, rows, lanes), f32),
            vmem((2, phases, 1, lanes), f32),
            vmem((total, lanes), f32),
            vmem((total, lanes), f32),
            vmem((2 * total, lanes), bf16),
            vmem((2 * total, lanes), bf16),
            vmem((phases, side, lanes), bf16),
            vmem((phases, side, lanes), bf16),
            vmem((phases, YS, side, lanes), f32),
            vmem((phases, rows, lanes), f32),
            vmem((phases, zs, rows, lanes), bf16),
            vmem((phases, zs - 1, rows, lanes), bf16),
            dma((phases, zs - 1)), dma((phases, zs - 1)),
            dma((phases,)), dma((phases,)),
            dma((phases,)), dma((phases,)),
            dma((phases, zs - 1)), dma((phases, zs - 1)),
            dma((2,)), dma((2,)), dma((2,)), dma((2,)), dma((phases,)),
        ],
        compiler_params=pltpu.CompilerParams(
            collective_id=0, has_side_effects=True, vmem_limit_bytes=56 << 20
        ),
    )(position, maps, kspace_data[0], sample_mask.T, jnp.asarray(rf), jnp.asarray(rb), jnp.asarray(wf), jnp.asarray(wb))


def with_halo(block, sides, width):
    for axis, dim in sides:
        count = lax.axis_size(axis)
        forward = [(i, i + 1) for i in range(count - 1)]
        forward.append((count - 1, 0))
        backward = [(target, source) for source, target in forward]
        low = lax.ppermute(
            lax.slice_in_dim(block, block.shape[dim] - width, None, axis=dim), axis, forward
        )
        high = lax.ppermute(lax.slice_in_dim(block, 0, width, axis=dim), axis, backward)
        block = jnp.concatenate([low, block, high], axis=dim)
    return block


def complex_times(factor, values, conjugate):
    width = values.shape[-1] // 2
    factor_real = factor[..., :width]
    factor_imag = factor[..., width:]
    if conjugate:
        factor_imag = -factor_imag
    value_real = values[..., :width]
    value_imag = values[..., width:]
    out_real = factor_real * value_real - factor_imag * value_imag
    out_imag = factor_real * value_imag + factor_imag * value_real
    return jnp.concatenate([out_real, out_imag], -1)


def rows_apply(table_real, table_imag, values, adjoint):
    width = values.shape[-1] // 2
    real_part = jnp.einsum("kn,npsd->kpsd", table_real, values, preferred_element_type=jnp.float32)
    imag_part = jnp.einsum("kn,npsd->kpsd", table_imag, values, preferred_element_type=jnp.float32)
    if adjoint:
        out_real = real_part[..., :width] + imag_part[..., width:]
        out_imag = real_part[..., width:] - imag_part[..., :width]
    else:
        out_real = real_part[..., :width] - imag_part[..., width:]
        out_imag = real_part[..., width:] + imag_part[..., :width]
    return jnp.concatenate([out_real, out_imag], -1)


def general(position, coil_maps, kspace_data, sample_mask):
    rows_total = coil_maps.shape[1]
    width = position.shape[3] // 2
    row_real, row_imag = (jnp.asarray(t) for t in row_tables(rows_total))
    forward_wide, backward_wide = (jnp.asarray(t) for t in wide_tables(width))
    coil_data = kspace_data[0]
    sample_weight = sample_mask.astype(jnp.float32)[:, :, None, None]
    position_low = position.astype(jnp.bfloat16)
    map_rows = coil_maps[0].astype(jnp.float32)[:, None]
    image = lax.all_gather(position_low, "coil", axis=0, tiled=True)
    lifted = complex_times(map_rows, image.astype(jnp.float32), False).astype(jnp.bfloat16)
    spread = jnp.einsum(
        "npsc,cd->npsd", lifted, forward_wide, preferred_element_type=jnp.float32
    ).astype(jnp.bfloat16)
    kspace = rows_apply(row_real, row_imag, spread, False)
    residual = (sample_weight * (kspace - coil_data.astype(jnp.float32))).astype(jnp.bfloat16)
    back_rows = rows_apply(row_real, row_imag, residual, True).astype(jnp.bfloat16)
    back = jnp.einsum("npsc,cd->npsd", back_rows, backward_wide, preferred_element_type=jnp.float32)
    likelihood = lax.psum_scatter(
        complex_times(map_rows, back, True), "coil", scatter_dimension=0, tiled=True
    )
    padded = with_halo(position, (("coil", 0), ("phase", 1)), 1)
    phase_part = 2.0 * position - padded[1:-1, :-2] - padded[1:-1, 2:]
    row_part = 2.0 * position - padded[:-2, 1:-1] - padded[2:, 1:-1]
    return 0.6 * likelihood + 0.5 * phase_part + 0.3 * row_part


def local(position, coil_maps, kspace_data, sample_mask):
    rows = position.shape[0]
    coils = lax.axis_size("coil")
    if coils == 8 and rows % 16 == 0 and position.shape[3] % 128 == 0:
        return fused(position, coil_maps, kspace_data, sample_mask)
    return general(position, coil_maps, kspace_data, sample_mask)


def solution(mesh):
    in_specs = (
        P("coil", "phase", "particle", None),
        P("coil", None, "particle", None),
        P("coil", None, "phase", "particle", None),
        P(None, "phase"),
    )
    out_specs = P("coil", "phase", "particle", None)
    return jax.shard_map(local, mesh=mesh, in_specs=in_specs, out_specs=out_specs, check_vma=False)
```

```python
import functools
import math

import jax
import jax.numpy as jnp
import ml_dtypes
import numpy as np
from jax import lax
from jax.experimental import pallas as pl
from jax.experimental.pallas import tpu as pltpu
from jax.sharding import PartitionSpec as P

MESH = pl.DeviceIdType.MESH
YS = 2


def dft_tables(length):
    counter = np.arange(length, dtype=np.int32)
    product = counter[:, None] * counter[None, :] % length
    angles = product.astype(np.float32) * np.float32(2.0 * math.pi / length)
    scaling = np.float32(1.0 / math.sqrt(length))
    return (np.cos(angles) * scaling, -np.sin(angles) * scaling)


def wide_tables(width):
    col_real, col_imag = dft_tables(width)
    forward = np.block([[col_real, col_imag], [-col_imag, col_real]])
    backward = np.block([[col_real, -col_imag], [col_imag, col_real]])
    return forward.astype(ml_dtypes.bfloat16), backward.astype(ml_dtypes.bfloat16)


def row_tables(rows_total):
    row_real, row_imag = dft_tables(rows_total)
    return row_real.astype(ml_dtypes.bfloat16), row_imag.astype(ml_dtypes.bfloat16)


def kernel(
    zs, phases, rows, width,
    pos_ref, map_ref, data_hbm, mask_ref, rf_ref, rb_ref, wf_ref, wb_ref,
    out_ref,
    data, edge, mask, low, gath, posx, halo_rows, fac_a, fac_b, vv, rr, ysend, yrecv, pown, own, zsend, zmid, zrecv,
    agz_s, agz_r, agy_s, agy_r, rsy_s, rsy_r, rsz_s, rsz_r, rsm_s, rsm_r, ph_s, ph_r, hr_s, hr_r, data_s,
):
    half = width // 2
    slices = pos_ref.shape[2]
    lanes = slices * width
    side = zs * rows
    total = YS * side
    coils = zs * YS
    coil = lax.axis_index("coil")
    z = coil // YS
    y = coil % YS
    other_y = 1 - y
    partner = z * YS + other_y
    phase_count = lax.axis_size("phase")
    ph = lax.axis_index("phase")
    ph_next = lax.rem(ph + 1, phase_count)
    ph_prev = lax.rem(ph + phase_count - 1, phase_count)
    c_next = lax.rem(coil + 1, coils)
    c_prev = lax.rem(coil + coils - 1, coils)
    z_to = [lax.rem(z + j, zs) for j in range(1, zs)]

    away = z // 2
    inner = (z == 1) | (z == 2)
    outer = (z == 0) | (z == 3)
    mate = away * 2 + 1 - z % 2
    facing = 2 - away
    opp = (1 - away) * 2
    columns = (y, other_y)

    def swapped(p):
        return p % 4 == 2

    def straight(p):
        return p % 4 != 2

    barrier = pltpu.get_barrier_semaphore()
    peers = [{"coil": t * YS + y} for t in z_to] + [{"coil": partner}]
    peers += [{"coil": c_next}, {"coil": c_prev}, {"phase": ph_next}, {"phase": ph_prev}]
    for peer in peers:
        pl.semaphore_signal(barrier, inc=1, device_id=peer, device_id_type=MESH)

    def data_copy(p):
        return pltpu.make_async_copy(data_hbm.at[:, p], data.at[p], data_s.at[p])

    @pl.loop(0, phases)
    def _(p):
        data_copy(p).start()
        for s in range(slices):
            cols = slice(s * width, (s + 1) * width)
            posx[p + 1, :, cols] = pos_ref[:, p, s, :]
        here = posx[p + 1]
        edge[0, p] = here[:1]
        edge[1, p] = here[rows - 1:]
        low[p] = here.astype(jnp.bfloat16)
        gath[p, y, z] = low[p]

    pl.semaphore_wait(barrier, len(peers))

    def ag_z(p, col, src, to, slot):
        return pltpu.make_async_remote_copy(
            src_ref=gath.at[p, col, src], dst_ref=gath.at[p, col, src],
            send_sem=agz_s.at[p, col, slot], recv_sem=agz_r.at[p, col, src],
            device_id={"coil": to * YS + y}, device_id_type=MESH,
        )

    def ag_own(p, col):
        return [ag_z(p, col, z, mate, 0), ag_z(p, col, z, facing, 1)]

    def ag_relay(p, col):
        return [ag_z(p, col, opp + k, mate, 2 + k) for k in range(2)]

    def wait_opp(p, col):
        for k in range(2):
            ag_z(p, col, opp + k, mate, 2 + k).wait_recv()

    def wait_mate(p, col):
        ag_z(p, col, mate, mate, 0).wait_recv()

    def ag_y(p):
        return pltpu.make_async_remote_copy(
            src_ref=gath.at[p, y], dst_ref=gath.at[p, y],
            send_sem=agy_s.at[p], recv_sem=agy_r.at[p],
            device_id={"coil": partner}, device_id_type=MESH,
        )

    def ag_y_one(p):
        return pltpu.make_async_remote_copy(
            src_ref=gath.at[p, y, z], dst_ref=gath.at[p, y, z],
            send_sem=agy_s.at[p], recv_sem=agy_r.at[p],
            device_id={"coil": partner}, device_id_type=MESH,
        )

    def rs_y_one(p):
        return pltpu.make_async_remote_copy(
            src_ref=ysend.at[p, pl.ds(0, rows)], dst_ref=yrecv.at[p, pl.ds(0, rows)],
            send_sem=rsy_s.at[p], recv_sem=rsy_r.at[p],
            device_id={"coil": partner}, device_id_type=MESH,
        )

    def rs_mate(p, col):
        return pltpu.make_async_remote_copy(
            src_ref=zsend.at[p, col, mate], dst_ref=zrecv.at[p, col, 0],
            send_sem=rsz_s.at[p, col, 0], recv_sem=rsz_r.at[p, col, 0],
            device_id={"coil": mate * YS + y}, device_id_type=MESH,
        )

    def rs_mid(p, col):
        return pltpu.make_async_remote_copy(
            src_ref=zsend.at[p, col, pl.ds(opp, 2)], dst_ref=zmid.at[p, col],
            send_sem=rsm_s.at[p, col], recv_sem=rsm_r.at[p, col],
            device_id={"coil": mate * YS + y}, device_id_type=MESH,
        )

    def rs_cross(p, col, k):
        return pltpu.make_async_remote_copy(
            src_ref=zsend.at[p, col, opp + k], dst_ref=zrecv.at[p, col, 1],
            send_sem=rsz_s.at[p, col, 1 + k], recv_sem=rsz_r.at[p, col, 1],
            device_id={"coil": (opp + k) * YS + y}, device_id_type=MESH,
        )

    def rs_y(p):
        return pltpu.make_async_remote_copy(
            src_ref=ysend.at[p], dst_ref=yrecv.at[p],
            send_sem=rsy_s.at[p], recv_sem=rsy_r.at[p],
            device_id={"coil": partner}, device_id_type=MESH,
        )

    def halo_copies():
        yield pltpu.make_async_remote_copy(
            src_ref=posx.at[phases], dst_ref=posx.at[0],
            send_sem=ph_s.at[0], recv_sem=ph_r.at[0],
            device_id={"phase": ph_next}, device_id_type=MESH,
        )
        yield pltpu.make_async_remote_copy(
            src_ref=posx.at[1], dst_ref=posx.at[phases + 1],
            send_sem=ph_s.at[1], recv_sem=ph_r.at[1],
            device_id={"phase": ph_prev}, device_id_type=MESH,
        )
        yield pltpu.make_async_remote_copy(
            src_ref=edge.at[1], dst_ref=halo_rows.at[0],
            send_sem=hr_s.at[0], recv_sem=hr_r.at[0],
            device_id={"coil": c_next}, device_id_type=MESH,
        )
        yield pltpu.make_async_remote_copy(
            src_ref=edge.at[0], dst_ref=halo_rows.at[1],
            send_sem=hr_s.at[1], recv_sem=hr_r.at[1],
            device_id={"coil": c_prev}, device_id_type=MESH,
        )

    @pl.loop(0, phases)
    def _(p):
        for copy in ag_own(p, y):
            copy.start()

        @pl.when(swapped(p))
        def _():
            ag_y_one(p).start()

    for copy in halo_copies():
        copy.start()

    first = lax.broadcasted_iota(jnp.int32, (total, width), 1) < half
    for s in range(slices):
        cols = slice(s * width, (s + 1) * width)
        plain = jnp.concatenate(
            [map_ref[pl.ds((b % zs * YS + b // zs) * rows, rows), cols] for b in range(coils)], 0
        ).astype(jnp.float32)
        turned = pltpu.roll(plain, half, 1)
        fac_a[:, cols] = jnp.where(first, plain, turned)
        fac_b[:, cols] = jnp.where(first, -turned, plain)

    mask[...] = mask_ref[...].astype(jnp.float32).T

    def gather_one(p):
        @pl.when(straight(p) & inner)
        def _():
            wait_opp(p, y)
            for copy in ag_relay(p, y):
                copy.start()

        @pl.when(swapped(p))
        def _():
            ag_y_one(p).wait_recv()
            for copy in ag_own(p, other_y):
                copy.start()

    def gather_two(p):
        @pl.when(straight(p))
        def _():
            @pl.when(outer)
            def _():
                wait_opp(p, y)

            wait_mate(p, y)
            ag_y(p).start()

        @pl.when(swapped(p) & inner)
        def _():
            for col in columns:
                wait_opp(p, col)
                for copy in ag_relay(p, col):
                    copy.start()

    def gather_end(p):
        @pl.when(straight(p))
        def _():
            ag_y(p).wait_recv()

        @pl.when(swapped(p))
        def _():
            @pl.when(outer)
            def _():
                for col in columns:
                    wait_opp(p, col)

            for col in columns:
                wait_mate(p, col)

    def compute(p):
        for s in range(slices):
            cols = slice(s * width, (s + 1) * width)
            x = gath[p, :, :, :, cols].reshape(total, width).astype(jnp.float32)
            lifted = fac_a[:, cols] * x + fac_b[:, cols] * pltpu.roll(x, half, 1)
            spread = jnp.dot(
                lifted.astype(jnp.bfloat16), wf_ref[...], preferred_element_type=jnp.float32
            ).astype(jnp.bfloat16)
            vv[:total, cols] = spread[:, :width]
            vv[total:, cols] = spread[:, width:]
        lane = lax.broadcasted_iota(jnp.int32, mask.shape, 1)
        weight = jnp.sum(jnp.where(lane == p, mask[...], 0.0), axis=1, keepdims=True)
        data_copy(p).wait()
        for s in range(slices):
            cols = slice(s * width, (s + 1) * width)
            kspace = jnp.dot(rf_ref[...], vv[:, cols], preferred_element_type=jnp.float32)
            residual = weight * (kspace - data[p, :, s, :].astype(jnp.float32))
            turned = pltpu.roll(residual, half, 1)
            rr[:total, cols] = residual.astype(jnp.bfloat16)
            rr[total:, cols] = jnp.where(first, turned, -turned).astype(jnp.bfloat16)
        for s in range(slices):
            cols = slice(s * width, (s + 1) * width)
            back_rows = jnp.dot(
                rb_ref[...], rr[:, cols], preferred_element_type=jnp.float32
            ).astype(jnp.bfloat16)
            back = jnp.dot(back_rows, wb_ref[...], preferred_element_type=jnp.float32)
            pown[p, :, :, cols] = (
                fac_a[:, cols] * back[:, :width] - fac_b[:, cols] * back[:, width:]
            ).reshape(YS, side, width)

    def send_rows(p, col):
        zsend[p, col] = pown[p, col].astype(jnp.bfloat16).reshape(zs, rows, lanes)
        rs_mate(p, col).start()

        @pl.when(outer)
        def _():
            rs_mid(p, col).start()

    def cross_rows(p, col):
        rs_mid(p, col).wait_recv()
        for k in range(2):
            at = pl.ds(pl.multiple_of((opp + k) * rows, rows), rows)
            both = pown[p, col, at, :] + zmid[p, col, k].astype(jnp.float32)
            zsend[p, col, opp + k] = both.astype(jnp.bfloat16)
            rs_cross(p, col, k).start()

    def own_rows(p, col):
        rs_mate(p, col).wait_recv()
        rs_cross(p, col, 0).wait_recv()
        mine = pown[p, col, pl.ds(pl.multiple_of(z * rows, rows), rows), :]
        return mine + zrecv[p, col, 0].astype(jnp.float32) + zrecv[p, col, 1].astype(jnp.float32)

    def reduce_start(p):
        @pl.when(straight(p))
        def _():
            ysend[p] = pown[p, other_y].astype(jnp.bfloat16)
            rs_y(p).start()

        @pl.when(swapped(p))
        def _():
            for col in columns:
                send_rows(p, col)

    def reduce_one(p):
        @pl.when(straight(p))
        def _():
            rs_y(p).wait_recv()
            pown[p, y] = pown[p, y] + yrecv[p].astype(jnp.float32)
            send_rows(p, y)

        @pl.when(swapped(p) & inner)
        def _():
            for col in columns:
                cross_rows(p, col)

    def reduce_two(p):
        @pl.when(straight(p) & inner)
        def _():
            cross_rows(p, y)

        @pl.when(swapped(p))
        def _():
            ysend[p, :rows] = own_rows(p, other_y).astype(jnp.bfloat16)
            rs_y_one(p).start()

    def during(p, step):
        @pl.when((p >= 0) & (p < phases))
        def _():
            step(p)

    @pl.loop(0, phases + 4)
    def _(t):
        during(t, gather_one)
        during(t - 1, gather_two)

        def whole(p):
            gather_end(p)
            compute(p)
            reduce_start(p)

        during(t - 2, whole)
        during(t - 3, reduce_one)
        during(t - 4, reduce_two)

    for copy in halo_copies():
        copy.wait()

    row = lax.broadcasted_iota(jnp.int32, (rows, lanes), 0)

    @pl.loop(0, phases)
    def _(p):
        own[p] = own_rows(p, y)

        @pl.when(swapped(p))
        def _():
            rs_y_one(p).wait_recv()
            own[p] = own[p] + yrecv[p, :rows].astype(jnp.float32)

        likelihood = own[p]
        here = posx[p + 1]
        phase_part = 2.0 * here - posx[p] - posx[p + 2]
        above = jnp.where(row == 0, halo_rows[0, p], pltpu.roll(here, 1, 0))
        below = jnp.where(row == rows - 1, halo_rows[1, p], pltpu.roll(here, rows - 1, 0))
        row_part = 2.0 * here - above - below
        grad = 0.6 * likelihood + 0.5 * phase_part + 0.3 * row_part
        for s in range(slices):
            out_ref[:, p, s, :] = grad[:, s * width : (s + 1) * width]

    @pl.loop(0, phases)
    def _(p):
        def column_sent(col):
            for copy in ag_own(p, col):
                copy.wait_send()
            rs_mate(p, col).wait_send()

            @pl.when(inner)
            def _():
                for k in range(2):
                    rs_cross(p, col, k).wait_send()
                for copy in ag_relay(p, col):
                    copy.wait_send()

            @pl.when(outer)
            def _():
                rs_mid(p, col).wait_send()

        column_sent(y)

        @pl.when(straight(p))
        def _():
            ag_y(p).wait_send()
            rs_y(p).wait_send()

        @pl.when(swapped(p))
        def _():
            column_sent(other_y)
            ag_y_one(p).wait_send()
            rs_y_one(p).wait_send()


def fused(position, coil_maps, kspace_data, sample_mask):
    rows, phases, slices, width = position.shape
    total = coil_maps.shape[1]
    zs = total // rows // YS
    side = zs * rows
    lanes = slices * width
    order = np.arange(total).reshape(zs, YS, rows).transpose(1, 0, 2).reshape(-1)
    row_real, row_imag = row_tables(total)
    rf = np.concatenate([row_real[:, order], row_imag[:, order]], 1)
    rb = np.concatenate([row_real[order], row_imag[order]], 1)
    forward, backward = wide_tables(width // 2)
    half = width // 2
    wf = np.concatenate([forward, -forward[:, half:], forward[:, :half]], 1)
    wb = np.concatenate([backward, backward[:, half:], backward[:, :half]], 1)

    maps = coil_maps[0].reshape(total, lanes)

    vmem = pltpu.VMEM
    bf16, f32 = jnp.bfloat16, jnp.float32
    dma = pltpu.SemaphoreType.DMA
    return pl.pallas_call(
        functools.partial(kernel, zs, phases, rows, width),
        out_shape=jax.ShapeDtypeStruct(position.shape, f32),
        in_specs=[pl.BlockSpec(memory_space=pl.ANY if i == 2 else vmem) for i in range(8)],
        out_specs=pl.BlockSpec(memory_space=vmem),
        scratch_shapes=[
            vmem((phases, total, slices, width), bf16),
            vmem((2, phases, 1, lanes), f32),
            vmem((total, phases), f32),
            vmem((phases, rows, lanes), bf16),
            vmem((phases, YS, zs, rows, lanes), bf16),
            vmem((phases + 2, rows, lanes), f32),
            vmem((2, phases, 1, lanes), f32),
            vmem((total, lanes), f32),
            vmem((total, lanes), f32),
            vmem((2 * total, lanes), bf16),
            vmem((2 * total, lanes), bf16),
            vmem((phases, side, lanes), bf16),
            vmem((phases, side, lanes), bf16),
            vmem((phases, YS, side, lanes), f32),
            vmem((phases, rows, lanes), f32),
            vmem((phases, YS, zs, rows, lanes), bf16),
            vmem((phases, YS, 2, rows, lanes), bf16),
            vmem((phases, YS, 2, rows, lanes), bf16),
            dma((phases, YS, 4)), dma((phases, YS, zs)),
            dma((phases,)), dma((phases,)),
            dma((phases,)), dma((phases,)),
            dma((phases, YS, 3)), dma((phases, YS, 2)),
            dma((phases, YS)), dma((phases, YS)),
            dma((2,)), dma((2,)), dma((2,)), dma((2,)), dma((phases,)),
        ],
        compiler_params=pltpu.CompilerParams(
            collective_id=0, has_side_effects=True, vmem_limit_bytes=56 << 20
        ),
    )(position, maps, kspace_data[0], sample_mask.T, jnp.asarray(rf), jnp.asarray(rb), jnp.asarray(wf), jnp.asarray(wb))


def with_halo(block, sides, width):
    for axis, dim in sides:
        count = lax.axis_size(axis)
        forward = [(i, i + 1) for i in range(count - 1)]
        forward.append((count - 1, 0))
        backward = [(target, source) for source, target in forward]
        low = lax.ppermute(
            lax.slice_in_dim(block, block.shape[dim] - width, None, axis=dim), axis, forward
        )
        high = lax.ppermute(lax.slice_in_dim(block, 0, width, axis=dim), axis, backward)
        block = jnp.concatenate([low, block, high], axis=dim)
    return block


def complex_times(factor, values, conjugate):
    width = values.shape[-1] // 2
    factor_real = factor[..., :width]
    factor_imag = factor[..., width:]
    if conjugate:
        factor_imag = -factor_imag
    value_real = values[..., :width]
    value_imag = values[..., width:]
    out_real = factor_real * value_real - factor_imag * value_imag
    out_imag = factor_real * value_imag + factor_imag * value_real
    return jnp.concatenate([out_real, out_imag], -1)


def rows_apply(table_real, table_imag, values, adjoint):
    width = values.shape[-1] // 2
    real_part = jnp.einsum("kn,npsd->kpsd", table_real, values, preferred_element_type=jnp.float32)
    imag_part = jnp.einsum("kn,npsd->kpsd", table_imag, values, preferred_element_type=jnp.float32)
    if adjoint:
        out_real = real_part[..., :width] + imag_part[..., width:]
        out_imag = real_part[..., width:] - imag_part[..., :width]
    else:
        out_real = real_part[..., :width] - imag_part[..., width:]
        out_imag = real_part[..., width:] + imag_part[..., :width]
    return jnp.concatenate([out_real, out_imag], -1)


def general(position, coil_maps, kspace_data, sample_mask):
    rows_total = coil_maps.shape[1]
    width = position.shape[3] // 2
    row_real, row_imag = (jnp.asarray(t) for t in row_tables(rows_total))
    forward_wide, backward_wide = (jnp.asarray(t) for t in wide_tables(width))
    coil_data = kspace_data[0]
    sample_weight = sample_mask.astype(jnp.float32)[:, :, None, None]
    position_low = position.astype(jnp.bfloat16)
    map_rows = coil_maps[0].astype(jnp.float32)[:, None]
    image = lax.all_gather(position_low, "coil", axis=0, tiled=True)
    lifted = complex_times(map_rows, image.astype(jnp.float32), False).astype(jnp.bfloat16)
    spread = jnp.einsum(
        "npsc,cd->npsd", lifted, forward_wide, preferred_element_type=jnp.float32
    ).astype(jnp.bfloat16)
    kspace = rows_apply(row_real, row_imag, spread, False)
    residual = (sample_weight * (kspace - coil_data.astype(jnp.float32))).astype(jnp.bfloat16)
    back_rows = rows_apply(row_real, row_imag, residual, True).astype(jnp.bfloat16)
    back = jnp.einsum("npsc,cd->npsd", back_rows, backward_wide, preferred_element_type=jnp.float32)
    likelihood = lax.psum_scatter(
        complex_times(map_rows, back, True), "coil", scatter_dimension=0, tiled=True
    )
    padded = with_halo(position, (("coil", 0), ("phase", 1)), 1)
    phase_part = 2.0 * position - padded[1:-1, :-2] - padded[1:-1, 2:]
    row_part = 2.0 * position - padded[:-2, 1:-1] - padded[2:, 1:-1]
    return 0.6 * likelihood + 0.5 * phase_part + 0.3 * row_part


def local(position, coil_maps, kspace_data, sample_mask):
    rows = position.shape[0]
    coils = lax.axis_size("coil")
    if coils == 8 and rows % 16 == 0 and position.shape[3] % 128 == 0:
        return fused(position, coil_maps, kspace_data, sample_mask)
    return general(position, coil_maps, kspace_data, sample_mask)


def solution(mesh):
    in_specs = (
        P("coil", "phase", "particle", None),
        P("coil", None, "particle", None),
        P("coil", None, "phase", "particle", None),
        P(None, "phase"),
    )
    out_specs = P("coil", "phase", "particle", None)
    return jax.shard_map(local, mesh=mesh, in_specs=in_specs, out_specs=out_specs, check_vma=False)
```

```python
import functools
import math

import jax
import jax.numpy as jnp
import ml_dtypes
import numpy as np
from jax import lax
from jax.experimental import pallas as pl
from jax.experimental.pallas import tpu as pltpu
from jax.sharding import PartitionSpec as P

MESH = pl.DeviceIdType.MESH
YS = 2


def dft_tables(length):
    counter = np.arange(length, dtype=np.int32)
    product = counter[:, None] * counter[None, :] % length
    angles = product.astype(np.float32) * np.float32(2.0 * math.pi / length)
    scaling = np.float32(1.0 / math.sqrt(length))
    return (np.cos(angles) * scaling, -np.sin(angles) * scaling)


def wide_tables(width):
    col_real, col_imag = dft_tables(width)
    forward = np.block([[col_real, col_imag], [-col_imag, col_real]])
    backward = np.block([[col_real, -col_imag], [col_imag, col_real]])
    return forward.astype(ml_dtypes.bfloat16), backward.astype(ml_dtypes.bfloat16)


def row_tables(rows_total):
    row_real, row_imag = dft_tables(rows_total)
    return row_real.astype(ml_dtypes.bfloat16), row_imag.astype(ml_dtypes.bfloat16)


def kernel(
    zs, phases, rows, width,
    pos_ref, map_ref, data_hbm, mask_ref, rf_ref, rb_ref, wf_ref, wb_ref,
    out_ref,
    data, edge, mask, low, gath, posx, halo_rows, fac_a, fac_b, vv, rr, ysend, yrecv, pown, own, zsend, zmid, zrecv,
    agz_s, agz_r, agy_s, agy_r, rsy_s, rsy_r, rsz_s, rsz_r, rsm_s, rsm_r, ph_s, ph_r, hr_s, hr_r, data_s,
):
    half = width // 2
    slices = pos_ref.shape[2]
    lanes = slices * width
    side = zs * rows
    total = YS * side
    coils = zs * YS
    coil = lax.axis_index("coil")
    z = coil // YS
    y = coil % YS
    other_y = 1 - y
    partner = z * YS + other_y
    phase_count = lax.axis_size("phase")
    ph = lax.axis_index("phase")
    ph_next = lax.rem(ph + 1, phase_count)
    ph_prev = lax.rem(ph + phase_count - 1, phase_count)
    c_next = lax.rem(coil + 1, coils)
    c_prev = lax.rem(coil + coils - 1, coils)
    z_to = [lax.rem(z + j, zs) for j in range(1, zs)]

    away = z // 2
    inner = (z == 1) | (z == 2)
    outer = (z == 0) | (z == 3)
    mate = away * 2 + 1 - z % 2
    facing = 2 - away
    opp = (1 - away) * 2
    columns = (y, other_y)

    def swapped(p):
        return p % 4 == 2

    def straight(p):
        return p % 4 != 2

    barrier = pltpu.get_barrier_semaphore()
    peers = [{"coil": t * YS + y} for t in z_to] + [{"coil": partner}]
    peers += [{"coil": c_next}, {"coil": c_prev}, {"phase": ph_next}, {"phase": ph_prev}]
    for peer in peers:
        pl.semaphore_signal(barrier, inc=1, device_id=peer, device_id_type=MESH)

    def data_copy(p):
        return pltpu.make_async_copy(data_hbm.at[:, p], data.at[p], data_s.at[p])

    @pl.loop(0, phases)
    def _(p):
        data_copy(p).start()
        for s in range(slices):
            cols = slice(s * width, (s + 1) * width)
            posx[p + 1, :, cols] = pos_ref[:, p, s, :]
        here = posx[p + 1]
        edge[0, p] = here[:1]
        edge[1, p] = here[rows - 1:]
        low[p] = here.astype(jnp.bfloat16)
        gath[p, y, z] = low[p]

    pl.semaphore_wait(barrier, len(peers))

    def ag_z(p, col, src, to, slot):
        return pltpu.make_async_remote_copy(
            src_ref=gath.at[p, col, src], dst_ref=gath.at[p, col, src],
            send_sem=agz_s.at[p, col, slot], recv_sem=agz_r.at[p, col, src],
            device_id={"coil": to * YS + y}, device_id_type=MESH,
        )

    def ag_own(p, col):
        return [ag_z(p, col, z, mate, 0), ag_z(p, col, z, facing, 1)]

    def ag_relay(p, col):
        return [ag_z(p, col, opp + k, mate, 2 + k) for k in range(2)]

    def wait_opp(p, col):
        for k in range(2):
            ag_z(p, col, opp + k, mate, 2 + k).wait_recv()

    def wait_mate(p, col):
        ag_z(p, col, mate, mate, 0).wait_recv()

    def ag_y(p, src):
        return pltpu.make_async_remote_copy(
            src_ref=gath.at[p, y, src], dst_ref=gath.at[p, y, src],
            send_sem=agy_s.at[p, src], recv_sem=agy_r.at[p, src],
            device_id={"coil": partner}, device_id_type=MESH,
        )

    def rs_y_one(p):
        return pltpu.make_async_remote_copy(
            src_ref=ysend.at[p, pl.ds(0, rows)], dst_ref=yrecv.at[p, pl.ds(0, rows)],
            send_sem=rsy_s.at[p], recv_sem=rsy_r.at[p],
            device_id={"coil": partner}, device_id_type=MESH,
        )

    def rs_mate(p, col):
        return pltpu.make_async_remote_copy(
            src_ref=zsend.at[p, col, mate], dst_ref=zrecv.at[p, col, 0],
            send_sem=rsz_s.at[p, col, 0], recv_sem=rsz_r.at[p, col, 0],
            device_id={"coil": mate * YS + y}, device_id_type=MESH,
        )

    def rs_mid(p, col):
        return pltpu.make_async_remote_copy(
            src_ref=zsend.at[p, col, pl.ds(opp, 2)], dst_ref=zmid.at[p, col],
            send_sem=rsm_s.at[p, col], recv_sem=rsm_r.at[p, col],
            device_id={"coil": mate * YS + y}, device_id_type=MESH,
        )

    def rs_cross(p, col, k):
        return pltpu.make_async_remote_copy(
            src_ref=zsend.at[p, col, opp + k], dst_ref=zrecv.at[p, col, 1],
            send_sem=rsz_s.at[p, col, 1 + k], recv_sem=rsz_r.at[p, col, 1],
            device_id={"coil": (opp + k) * YS + y}, device_id_type=MESH,
        )

    def rs_y(p):
        return pltpu.make_async_remote_copy(
            src_ref=ysend.at[p], dst_ref=yrecv.at[p],
            send_sem=rsy_s.at[p], recv_sem=rsy_r.at[p],
            device_id={"coil": partner}, device_id_type=MESH,
        )

    def halo_copies():
        yield pltpu.make_async_remote_copy(
            src_ref=posx.at[phases], dst_ref=posx.at[0],
            send_sem=ph_s.at[0], recv_sem=ph_r.at[0],
            device_id={"phase": ph_next}, device_id_type=MESH,
        )
        yield pltpu.make_async_remote_copy(
            src_ref=posx.at[1], dst_ref=posx.at[phases + 1],
            send_sem=ph_s.at[1], recv_sem=ph_r.at[1],
            device_id={"phase": ph_prev}, device_id_type=MESH,
        )
        yield pltpu.make_async_remote_copy(
            src_ref=edge.at[1], dst_ref=halo_rows.at[0],
            send_sem=hr_s.at[0], recv_sem=hr_r.at[0],
            device_id={"coil": c_next}, device_id_type=MESH,
        )
        yield pltpu.make_async_remote_copy(
            src_ref=edge.at[0], dst_ref=halo_rows.at[1],
            send_sem=hr_s.at[1], recv_sem=hr_r.at[1],
            device_id={"coil": c_prev}, device_id_type=MESH,
        )

    @pl.loop(0, phases)
    def _(p):
        for copy in ag_own(p, y):
            copy.start()

        @pl.when(swapped(p))
        def _():
            ag_y(p, z).start()

    for copy in halo_copies():
        copy.start()

    first = lax.broadcasted_iota(jnp.int32, (total, width), 1) < half
    for s in range(slices):
        cols = slice(s * width, (s + 1) * width)
        plain = jnp.concatenate(
            [map_ref[pl.ds((b % zs * YS + b // zs) * rows, rows), s, :] for b in range(coils)], 0
        ).astype(jnp.float32)
        turned = pltpu.roll(plain, half, 1)
        fac_a[:, cols] = jnp.where(first, plain, turned)
        fac_b[:, cols] = jnp.where(first, -turned, plain)

    mask[...] = mask_ref[...].astype(jnp.float32).T

    def gather_one(p):
        @pl.when(straight(p))
        def _():
            ag_y(p, z).start()

        @pl.when(straight(p) & inner)
        def _():
            wait_opp(p, y)
            for copy in ag_relay(p, y):
                copy.start()
            for k in range(2):
                ag_y(p, opp + k).start()

        @pl.when(swapped(p))
        def _():
            ag_y(p, z).wait_recv()
            for copy in ag_own(p, other_y):
                copy.start()

    def gather_two(p):
        @pl.when(straight(p))
        def _():
            @pl.when(outer)
            def _():
                wait_opp(p, y)
                for k in range(2):
                    ag_y(p, opp + k).start()

            wait_mate(p, y)
            ag_y(p, mate).start()

        @pl.when(swapped(p) & inner)
        def _():
            for col in columns:
                wait_opp(p, col)
                for copy in ag_relay(p, col):
                    copy.start()

    def gather_end(p):
        @pl.when(straight(p))
        def _():
            for k in range(zs):
                ag_y(p, k).wait_recv()

        @pl.when(swapped(p))
        def _():
            @pl.when(outer)
            def _():
                for col in columns:
                    wait_opp(p, col)

            for col in columns:
                wait_mate(p, col)

    def compute(p):
        for s in range(slices):
            cols = slice(s * width, (s + 1) * width)
            x = gath[p, :, :, :, cols].reshape(total, width).astype(jnp.float32)
            lifted = fac_a[:, cols] * x + fac_b[:, cols] * pltpu.roll(x, half, 1)
            spread = jnp.dot(
                lifted.astype(jnp.bfloat16), wf_ref[...], preferred_element_type=jnp.float32
            ).astype(jnp.bfloat16)
            vv[:total, cols] = spread[:, :width]
            vv[total:, cols] = spread[:, width:]
        lane = lax.broadcasted_iota(jnp.int32, mask.shape, 1)
        weight = jnp.sum(jnp.where(lane == p, mask[...], 0.0), axis=1, keepdims=True)
        data_copy(p).wait()
        for s in range(slices):
            cols = slice(s * width, (s + 1) * width)
            kspace = jnp.dot(rf_ref[...], vv[:, cols], preferred_element_type=jnp.float32)
            residual = weight * (kspace - data[p, :, s, :].astype(jnp.float32))
            turned = pltpu.roll(residual, half, 1)
            rr[:total, cols] = residual.astype(jnp.bfloat16)
            rr[total:, cols] = jnp.where(first, turned, -turned).astype(jnp.bfloat16)
        for s in range(slices):
            cols = slice(s * width, (s + 1) * width)
            back_rows = jnp.dot(
                rb_ref[...], rr[:, cols], preferred_element_type=jnp.float32
            ).astype(jnp.bfloat16)
            back = jnp.dot(back_rows, wb_ref[...], preferred_element_type=jnp.float32)
            pown[p, :, :, cols] = (
                fac_a[:, cols] * back[:, :width] - fac_b[:, cols] * back[:, width:]
            ).reshape(YS, side, width)

    def send_rows(p, col):
        zsend[p, col] = pown[p, col].astype(jnp.bfloat16).reshape(zs, rows, lanes)
        rs_mate(p, col).start()

        @pl.when(outer)
        def _():
            rs_mid(p, col).start()

    def cross_rows(p, col):
        rs_mid(p, col).wait_recv()
        for k in range(2):
            at = pl.ds(pl.multiple_of((opp + k) * rows, rows), rows)
            both = pown[p, col, at, :] + zmid[p, col, k].astype(jnp.float32)
            zsend[p, col, opp + k] = both.astype(jnp.bfloat16)
            rs_cross(p, col, k).start()

    def own_rows(p, col):
        rs_mate(p, col).wait_recv()
        rs_cross(p, col, 0).wait_recv()
        mine = pown[p, col, pl.ds(pl.multiple_of(z * rows, rows), rows), :]
        return mine + zrecv[p, col, 0].astype(jnp.float32) + zrecv[p, col, 1].astype(jnp.float32)

    def reduce_start(p):
        @pl.when(straight(p))
        def _():
            ysend[p] = pown[p, other_y].astype(jnp.bfloat16)
            rs_y(p).start()

        @pl.when(swapped(p))
        def _():
            for col in columns:
                send_rows(p, col)

    def reduce_one(p):
        @pl.when(straight(p))
        def _():
            rs_y(p).wait_recv()
            pown[p, y] = pown[p, y] + yrecv[p].astype(jnp.float32)
            send_rows(p, y)

        @pl.when(swapped(p) & inner)
        def _():
            for col in columns:
                cross_rows(p, col)

    def reduce_two(p):
        @pl.when(straight(p) & inner)
        def _():
            cross_rows(p, y)

        @pl.when(swapped(p))
        def _():
            ysend[p, :rows] = own_rows(p, other_y).astype(jnp.bfloat16)
            rs_y_one(p).start()

    def during(p, step):
        @pl.when((p >= 0) & (p < phases))
        def _():
            step(p)

    @pl.loop(0, phases + 4)
    def _(t):
        during(t, gather_one)
        during(t - 1, gather_two)

        def whole(p):
            gather_end(p)
            compute(p)
            reduce_start(p)

        during(t - 2, whole)
        during(t - 3, reduce_one)
        during(t - 4, reduce_two)

    for copy in halo_copies():
        copy.wait()

    row = lax.broadcasted_iota(jnp.int32, (rows, lanes), 0)

    @pl.loop(0, phases)
    def _(p):
        own[p] = own_rows(p, y)

        @pl.when(swapped(p))
        def _():
            rs_y_one(p).wait_recv()
            own[p] = own[p] + yrecv[p, :rows].astype(jnp.float32)

        likelihood = own[p]
        here = posx[p + 1]
        phase_part = 2.0 * here - posx[p] - posx[p + 2]
        above = jnp.where(row == 0, halo_rows[0, p], pltpu.roll(here, 1, 0))
        below = jnp.where(row == rows - 1, halo_rows[1, p], pltpu.roll(here, rows - 1, 0))
        row_part = 2.0 * here - above - below
        grad = 0.6 * likelihood + 0.5 * phase_part + 0.3 * row_part
        for s in range(slices):
            out_ref[:, p, s, :] = grad[:, s * width : (s + 1) * width]

    @pl.loop(0, phases)
    def _(p):
        def column_sent(col):
            for copy in ag_own(p, col):
                copy.wait_send()
            rs_mate(p, col).wait_send()

            @pl.when(inner)
            def _():
                for k in range(2):
                    rs_cross(p, col, k).wait_send()
                for copy in ag_relay(p, col):
                    copy.wait_send()

            @pl.when(outer)
            def _():
                rs_mid(p, col).wait_send()

        column_sent(y)

        @pl.when(straight(p))
        def _():
            for k in range(zs):
                ag_y(p, k).wait_send()
            rs_y(p).wait_send()

        @pl.when(swapped(p))
        def _():
            column_sent(other_y)
            ag_y(p, z).wait_send()
            rs_y_one(p).wait_send()


def fused(position, coil_maps, kspace_data, sample_mask):
    rows, phases, slices, width = position.shape
    total = coil_maps.shape[1]
    zs = total // rows // YS
    side = zs * rows
    lanes = slices * width
    order = np.arange(total).reshape(zs, YS, rows).transpose(1, 0, 2).reshape(-1)
    row_real, row_imag = row_tables(total)
    rf = np.concatenate([row_real[:, order], row_imag[:, order]], 1)
    rb = np.concatenate([row_real[order], row_imag[order]], 1)
    forward, backward = wide_tables(width // 2)
    half = width // 2
    wf = np.concatenate([forward, -forward[:, half:], forward[:, :half]], 1)
    wb = np.concatenate([backward, backward[:, half:], backward[:, :half]], 1)


    vmem = pltpu.VMEM
    bf16, f32 = jnp.bfloat16, jnp.float32
    dma = pltpu.SemaphoreType.DMA
    return pl.pallas_call(
        functools.partial(kernel, zs, phases, rows, width),
        out_shape=jax.ShapeDtypeStruct(position.shape, f32),
        in_specs=[pl.BlockSpec(memory_space=pl.ANY if i == 2 else vmem) for i in range(8)],
        out_specs=pl.BlockSpec(memory_space=vmem),
        scratch_shapes=[
            vmem((phases, total, slices, width), bf16),
            vmem((2, phases, 1, lanes), f32),
            vmem((total, phases), f32),
            vmem((phases, rows, lanes), bf16),
            vmem((phases, YS, zs, rows, lanes), bf16),
            vmem((phases + 2, rows, lanes), f32),
            vmem((2, phases, 1, lanes), f32),
            vmem((total, lanes), f32),
            vmem((total, lanes), f32),
            vmem((2 * total, lanes), bf16),
            vmem((2 * total, lanes), bf16),
            vmem((phases, side, lanes), bf16),
            vmem((phases, side, lanes), bf16),
            vmem((phases, YS, side, lanes), f32),
            vmem((phases, rows, lanes), f32),
            vmem((phases, YS, zs, rows, lanes), bf16),
            vmem((phases, YS, 2, rows, lanes), bf16),
            vmem((phases, YS, 2, rows, lanes), bf16),
            dma((phases, YS, 4)), dma((phases, YS, zs)),
            dma((phases, zs)), dma((phases, zs)),
            dma((phases,)), dma((phases,)),
            dma((phases, YS, 3)), dma((phases, YS, 2)),
            dma((phases, YS)), dma((phases, YS)),
            dma((2,)), dma((2,)), dma((2,)), dma((2,)), dma((phases,)),
        ],
        compiler_params=pltpu.CompilerParams(
            collective_id=0, has_side_effects=True, vmem_limit_bytes=56 << 20
        ),
    )(position, coil_maps[0], kspace_data[0], sample_mask.T, jnp.asarray(rf), jnp.asarray(rb), jnp.asarray(wf), jnp.asarray(wb))


def with_halo(block, sides, width):
    for axis, dim in sides:
        count = lax.axis_size(axis)
        forward = [(i, i + 1) for i in range(count - 1)]
        forward.append((count - 1, 0))
        backward = [(target, source) for source, target in forward]
        low = lax.ppermute(
            lax.slice_in_dim(block, block.shape[dim] - width, None, axis=dim), axis, forward
        )
        high = lax.ppermute(lax.slice_in_dim(block, 0, width, axis=dim), axis, backward)
        block = jnp.concatenate([low, block, high], axis=dim)
    return block


def complex_times(factor, values, conjugate):
    width = values.shape[-1] // 2
    factor_real = factor[..., :width]
    factor_imag = factor[..., width:]
    if conjugate:
        factor_imag = -factor_imag
    value_real = values[..., :width]
    value_imag = values[..., width:]
    out_real = factor_real * value_real - factor_imag * value_imag
    out_imag = factor_real * value_imag + factor_imag * value_real
    return jnp.concatenate([out_real, out_imag], -1)


def rows_apply(table_real, table_imag, values, adjoint):
    width = values.shape[-1] // 2
    real_part = jnp.einsum("kn,npsd->kpsd", table_real, values, preferred_element_type=jnp.float32)
    imag_part = jnp.einsum("kn,npsd->kpsd", table_imag, values, preferred_element_type=jnp.float32)
    if adjoint:
        out_real = real_part[..., :width] + imag_part[..., width:]
        out_imag = real_part[..., width:] - imag_part[..., :width]
    else:
        out_real = real_part[..., :width] - imag_part[..., width:]
        out_imag = real_part[..., width:] + imag_part[..., :width]
    return jnp.concatenate([out_real, out_imag], -1)


def general(position, coil_maps, kspace_data, sample_mask):
    rows_total = coil_maps.shape[1]
    width = position.shape[3] // 2
    row_real, row_imag = (jnp.asarray(t) for t in row_tables(rows_total))
    forward_wide, backward_wide = (jnp.asarray(t) for t in wide_tables(width))
    coil_data = kspace_data[0]
    sample_weight = sample_mask.astype(jnp.float32)[:, :, None, None]
    position_low = position.astype(jnp.bfloat16)
    map_rows = coil_maps[0].astype(jnp.float32)[:, None]
    image = lax.all_gather(position_low, "coil", axis=0, tiled=True)
    lifted = complex_times(map_rows, image.astype(jnp.float32), False).astype(jnp.bfloat16)
    spread = jnp.einsum(
        "npsc,cd->npsd", lifted, forward_wide, preferred_element_type=jnp.float32
    ).astype(jnp.bfloat16)
    kspace = rows_apply(row_real, row_imag, spread, False)
    residual = (sample_weight * (kspace - coil_data.astype(jnp.float32))).astype(jnp.bfloat16)
    back_rows = rows_apply(row_real, row_imag, residual, True).astype(jnp.bfloat16)
    back = jnp.einsum("npsc,cd->npsd", back_rows, backward_wide, preferred_element_type=jnp.float32)
    likelihood = lax.psum_scatter(
        complex_times(map_rows, back, True), "coil", scatter_dimension=0, tiled=True
    )
    padded = with_halo(position, (("coil", 0), ("phase", 1)), 1)
    phase_part = 2.0 * position - padded[1:-1, :-2] - padded[1:-1, 2:]
    row_part = 2.0 * position - padded[:-2, 1:-1] - padded[2:, 1:-1]
    return 0.6 * likelihood + 0.5 * phase_part + 0.3 * row_part


def local(position, coil_maps, kspace_data, sample_mask):
    rows = position.shape[0]
    coils = lax.axis_size("coil")
    if coils == 8 and rows % 16 == 0 and position.shape[3] % 128 == 0:
        return fused(position, coil_maps, kspace_data, sample_mask)
    return general(position, coil_maps, kspace_data, sample_mask)


def solution(mesh):
    in_specs = (
        P("coil", "phase", "particle", None),
        P("coil", None, "particle", None),
        P("coil", None, "phase", "particle", None),
        P(None, "phase"),
    )
    out_specs = P("coil", "phase", "particle", None)
    return jax.shard_map(local, mesh=mesh, in_specs=in_specs, out_specs=out_specs, check_vma=False)
```

```python
import functools
import math

import jax
import jax.numpy as jnp
import ml_dtypes
import numpy as np
from jax import lax
from jax.experimental import pallas as pl
from jax.experimental.pallas import tpu as pltpu
from jax.sharding import PartitionSpec as P

MESH = pl.DeviceIdType.MESH
YS = 2


def dft_tables(length):
    counter = np.arange(length, dtype=np.int32)
    product = counter[:, None] * counter[None, :] % length
    angles = product.astype(np.float32) * np.float32(2.0 * math.pi / length)
    scaling = np.float32(1.0 / math.sqrt(length))
    return (np.cos(angles) * scaling, -np.sin(angles) * scaling)


def wide_tables(width):
    col_real, col_imag = dft_tables(width)
    forward = np.block([[col_real, col_imag], [-col_imag, col_real]])
    backward = np.block([[col_real, -col_imag], [col_imag, col_real]])
    return forward.astype(ml_dtypes.bfloat16), backward.astype(ml_dtypes.bfloat16)


def row_tables(rows_total):
    row_real, row_imag = dft_tables(rows_total)
    return row_real.astype(ml_dtypes.bfloat16), row_imag.astype(ml_dtypes.bfloat16)


def kernel(
    zs, phases, rows, width,
    pos_ref, map_ref, data_hbm, mask_ref, rf_ref, rb_ref, wf_ref, wb_ref,
    out_ref,
    data, edge, mask, low, gath, posx, halo_rows, fac_a, fac_b, vv, rr, ysend, yrecv, pown, own, zsend, zmid, zrecv,
    agz_s, agz_r, agy_s, agy_r, rsy_s, rsy_r, rsz_s, rsz_r, rsm_s, rsm_r, ph_s, ph_r, hr_s, hr_r, data_s,
):
    half = width // 2
    slices = pos_ref.shape[2]
    lanes = slices * width
    side = zs * rows
    total = YS * side
    coils = zs * YS
    coil = lax.axis_index("coil")
    z = coil // YS
    y = coil % YS
    other_y = 1 - y
    partner = z * YS + other_y
    phase_count = lax.axis_size("phase")
    ph = lax.axis_index("phase")
    ph_next = lax.rem(ph + 1, phase_count)
    ph_prev = lax.rem(ph + phase_count - 1, phase_count)
    c_next = lax.rem(coil + 1, coils)
    c_prev = lax.rem(coil + coils - 1, coils)
    z_to = [lax.rem(z + j, zs) for j in range(1, zs)]

    away = z // 2
    inner = (z == 1) | (z == 2)
    outer = (z == 0) | (z == 3)
    mate = away * 2 + 1 - z % 2
    facing = 2 - away
    opp = (1 - away) * 2
    columns = (y, other_y)

    def swapped(p):
        return p % 4 == 2

    def straight(p):
        return p % 4 != 2

    barrier = pltpu.get_barrier_semaphore()
    peers = [{"coil": t * YS + y} for t in z_to] + [{"coil": partner}]
    peers += [{"coil": c_next}, {"coil": c_prev}, {"phase": ph_next}, {"phase": ph_prev}]
    for peer in peers:
        pl.semaphore_signal(barrier, inc=1, device_id=peer, device_id_type=MESH)

    def data_copy(p):
        return pltpu.make_async_copy(data_hbm.at[:, p], data.at[p], data_s.at[p])

    def prepare(p):
        data_copy(p).start()
        for s in range(slices):
            cols = slice(s * width, (s + 1) * width)
            posx[p + 1, :, cols] = pos_ref[:, p, s, :]
        here = posx[p + 1]
        edge[0, p] = here[:1]
        edge[1, p] = here[rows - 1:]
        low[p] = here.astype(jnp.bfloat16)
        gath[p, y, z] = low[p]

    prepare(0)
    pl.semaphore_wait(barrier, len(peers))

    def ag_z(p, col, src, to, slot):
        return pltpu.make_async_remote_copy(
            src_ref=gath.at[p, col, src], dst_ref=gath.at[p, col, src],
            send_sem=agz_s.at[p, col, slot], recv_sem=agz_r.at[p, col, src],
            device_id={"coil": to * YS + y}, device_id_type=MESH,
        )

    def ag_own(p, col):
        return [ag_z(p, col, z, mate, 0), ag_z(p, col, z, facing, 1)]

    def ag_relay(p, col):
        return [ag_z(p, col, opp + k, mate, 2 + k) for k in range(2)]

    def wait_opp(p, col):
        for k in range(2):
            ag_z(p, col, opp + k, mate, 2 + k).wait_recv()

    def wait_mate(p, col):
        ag_z(p, col, mate, mate, 0).wait_recv()

    def ag_y(p, src):
        return pltpu.make_async_remote_copy(
            src_ref=gath.at[p, y, src], dst_ref=gath.at[p, y, src],
            send_sem=agy_s.at[p, src], recv_sem=agy_r.at[p, src],
            device_id={"coil": partner}, device_id_type=MESH,
        )

    def rs_y_one(p):
        return pltpu.make_async_remote_copy(
            src_ref=ysend.at[p, pl.ds(0, rows)], dst_ref=yrecv.at[p, pl.ds(0, rows)],
            send_sem=rsy_s.at[p], recv_sem=rsy_r.at[p],
            device_id={"coil": partner}, device_id_type=MESH,
        )

    def rs_mate(p, col):
        return pltpu.make_async_remote_copy(
            src_ref=zsend.at[p, col, mate], dst_ref=zrecv.at[p, col, 0],
            send_sem=rsz_s.at[p, col, 0], recv_sem=rsz_r.at[p, col, 0],
            device_id={"coil": mate * YS + y}, device_id_type=MESH,
        )

    def rs_mid(p, col):
        return pltpu.make_async_remote_copy(
            src_ref=zsend.at[p, col, pl.ds(opp, 2)], dst_ref=zmid.at[p, col],
            send_sem=rsm_s.at[p, col], recv_sem=rsm_r.at[p, col],
            device_id={"coil": mate * YS + y}, device_id_type=MESH,
        )

    def rs_cross(p, col, k):
        return pltpu.make_async_remote_copy(
            src_ref=zsend.at[p, col, opp + k], dst_ref=zrecv.at[p, col, 1],
            send_sem=rsz_s.at[p, col, 1 + k], recv_sem=rsz_r.at[p, col, 1],
            device_id={"coil": (opp + k) * YS + y}, device_id_type=MESH,
        )

    def rs_y(p):
        return pltpu.make_async_remote_copy(
            src_ref=ysend.at[p], dst_ref=yrecv.at[p],
            send_sem=rsy_s.at[p], recv_sem=rsy_r.at[p],
            device_id={"coil": partner}, device_id_type=MESH,
        )

    def halo_copies():
        yield pltpu.make_async_remote_copy(
            src_ref=posx.at[phases], dst_ref=posx.at[0],
            send_sem=ph_s.at[0], recv_sem=ph_r.at[0],
            device_id={"phase": ph_next}, device_id_type=MESH,
        )
        yield pltpu.make_async_remote_copy(
            src_ref=posx.at[1], dst_ref=posx.at[phases + 1],
            send_sem=ph_s.at[1], recv_sem=ph_r.at[1],
            device_id={"phase": ph_prev}, device_id_type=MESH,
        )
        yield pltpu.make_async_remote_copy(
            src_ref=edge.at[1], dst_ref=halo_rows.at[0],
            send_sem=hr_s.at[0], recv_sem=hr_r.at[0],
            device_id={"coil": c_next}, device_id_type=MESH,
        )
        yield pltpu.make_async_remote_copy(
            src_ref=edge.at[0], dst_ref=halo_rows.at[1],
            send_sem=hr_s.at[1], recv_sem=hr_r.at[1],
            device_id={"coil": c_prev}, device_id_type=MESH,
        )

    @pl.loop(0, phases)
    def _(p):
        @pl.when(p > 0)
        def _():
            prepare(p)

        for copy in ag_own(p, y):
            copy.start()

        @pl.when(swapped(p))
        def _():
            ag_y(p, z).start()

    for copy in halo_copies():
        copy.start()

    first = lax.broadcasted_iota(jnp.int32, (total, width), 1) < half
    for s in range(slices):
        cols = slice(s * width, (s + 1) * width)
        plain = jnp.concatenate(
            [map_ref[pl.ds((b % zs * YS + b // zs) * rows, rows), s, :] for b in range(coils)], 0
        ).astype(jnp.float32)
        turned = pltpu.roll(plain, half, 1)
        fac_a[:, cols] = jnp.where(first, plain, turned)
        fac_b[:, cols] = jnp.where(first, -turned, plain)

    mask[...] = mask_ref[...].astype(jnp.float32).T

    def gather_one(p):
        @pl.when(straight(p))
        def _():
            ag_y(p, z).start()

        @pl.when(straight(p) & inner)
        def _():
            wait_opp(p, y)
            for copy in ag_relay(p, y):
                copy.start()
            for k in range(2):
                ag_y(p, opp + k).start()

        @pl.when(swapped(p))
        def _():
            ag_y(p, z).wait_recv()
            for copy in ag_own(p, other_y):
                copy.start()

    def gather_two(p):
        @pl.when(straight(p))
        def _():
            @pl.when(outer)
            def _():
                wait_opp(p, y)
                for k in range(2):
                    ag_y(p, opp + k).start()

            wait_mate(p, y)
            ag_y(p, mate).start()

        @pl.when(swapped(p) & inner)
        def _():
            for col in columns:
                wait_opp(p, col)
                for copy in ag_relay(p, col):
                    copy.start()

    def gather_end(p):
        @pl.when(straight(p))
        def _():
            for k in range(zs):
                ag_y(p, k).wait_recv()

        @pl.when(swapped(p))
        def _():
            @pl.when(outer)
            def _():
                for col in columns:
                    wait_opp(p, col)

            for col in columns:
                wait_mate(p, col)

    def compute(p):
        for s in range(slices):
            cols = slice(s * width, (s + 1) * width)
            x = gath[p, :, :, :, cols].reshape(total, width).astype(jnp.float32)
            lifted = fac_a[:, cols] * x + fac_b[:, cols] * pltpu.roll(x, half, 1)
            spread = jnp.dot(
                lifted.astype(jnp.bfloat16), wf_ref[...], preferred_element_type=jnp.float32
            ).astype(jnp.bfloat16)
            vv[:total, cols] = spread[:, :width]
            vv[total:, cols] = spread[:, width:]
        lane = lax.broadcasted_iota(jnp.int32, mask.shape, 1)
        weight = jnp.sum(jnp.where(lane == p, mask[...], 0.0), axis=1, keepdims=True)
        data_copy(p).wait()
        for s in range(slices):
            cols = slice(s * width, (s + 1) * width)
            kspace = jnp.dot(rf_ref[...], vv[:, cols], preferred_element_type=jnp.float32)
            residual = weight * (kspace - data[p, :, s, :].astype(jnp.float32))
            turned = pltpu.roll(residual, half, 1)
            rr[:total, cols] = residual.astype(jnp.bfloat16)
            rr[total:, cols] = jnp.where(first, turned, -turned).astype(jnp.bfloat16)
        for s in range(slices):
            cols = slice(s * width, (s + 1) * width)
            back_rows = jnp.dot(
                rb_ref[...], rr[:, cols], preferred_element_type=jnp.float32
            ).astype(jnp.bfloat16)
            back = jnp.dot(back_rows, wb_ref[...], preferred_element_type=jnp.float32)
            pown[p, :, :, cols] = (
                fac_a[:, cols] * back[:, :width] - fac_b[:, cols] * back[:, width:]
            ).reshape(YS, side, width)

    def send_rows(p, col):
        zsend[p, col] = pown[p, col].astype(jnp.bfloat16).reshape(zs, rows, lanes)
        rs_mate(p, col).start()

        @pl.when(outer)
        def _():
            rs_mid(p, col).start()

    def cross_rows(p, col):
        rs_mid(p, col).wait_recv()
        for k in range(2):
            at = pl.ds(pl.multiple_of((opp + k) * rows, rows), rows)
            both = pown[p, col, at, :] + zmid[p, col, k].astype(jnp.float32)
            zsend[p, col, opp + k] = both.astype(jnp.bfloat16)
            rs_cross(p, col, k).start()

    def own_rows(p, col):
        rs_mate(p, col).wait_recv()
        rs_cross(p, col, 0).wait_recv()
        mine = pown[p, col, pl.ds(pl.multiple_of(z * rows, rows), rows), :]
        return mine + zrecv[p, col, 0].astype(jnp.float32) + zrecv[p, col, 1].astype(jnp.float32)

    def reduce_start(p):
        @pl.when(straight(p))
        def _():
            ysend[p] = pown[p, other_y].astype(jnp.bfloat16)
            rs_y(p).start()

        @pl.when(swapped(p))
        def _():
            for col in columns:
                send_rows(p, col)

    def reduce_one(p):
        @pl.when(straight(p))
        def _():
            rs_y(p).wait_recv()
            pown[p, y] = pown[p, y] + yrecv[p].astype(jnp.float32)
            send_rows(p, y)

        @pl.when(swapped(p) & inner)
        def _():
            for col in columns:
                cross_rows(p, col)

    def reduce_two(p):
        @pl.when(straight(p) & inner)
        def _():
            cross_rows(p, y)

        @pl.when(swapped(p))
        def _():
            ysend[p, :rows] = own_rows(p, other_y).astype(jnp.bfloat16)
            rs_y_one(p).start()

    def during(p, step):
        @pl.when((p >= 0) & (p < phases))
        def _():
            step(p)

    @pl.loop(0, phases + 4)
    def _(t):
        during(t, gather_one)
        during(t - 1, gather_two)

        def whole(p):
            gather_end(p)
            compute(p)
            reduce_start(p)

        during(t - 2, whole)
        during(t - 3, reduce_one)
        during(t - 4, reduce_two)

    for copy in halo_copies():
        copy.wait()

    row = lax.broadcasted_iota(jnp.int32, (rows, lanes), 0)

    @pl.loop(0, phases)
    def _(p):
        own[p] = own_rows(p, y)

        @pl.when(swapped(p))
        def _():
            rs_y_one(p).wait_recv()
            own[p] = own[p] + yrecv[p, :rows].astype(jnp.float32)

        likelihood = own[p]
        here = posx[p + 1]
        phase_part = 2.0 * here - posx[p] - posx[p + 2]
        above = jnp.where(row == 0, halo_rows[0, p], pltpu.roll(here, 1, 0))
        below = jnp.where(row == rows - 1, halo_rows[1, p], pltpu.roll(here, rows - 1, 0))
        row_part = 2.0 * here - above - below
        grad = 0.6 * likelihood + 0.5 * phase_part + 0.3 * row_part
        for s in range(slices):
            out_ref[:, p, s, :] = grad[:, s * width : (s + 1) * width]

    @pl.loop(0, phases)
    def _(p):
        def column_sent(col):
            for copy in ag_own(p, col):
                copy.wait_send()
            rs_mate(p, col).wait_send()

            @pl.when(inner)
            def _():
                for k in range(2):
                    rs_cross(p, col, k).wait_send()
                for copy in ag_relay(p, col):
                    copy.wait_send()

            @pl.when(outer)
            def _():
                rs_mid(p, col).wait_send()

        column_sent(y)

        @pl.when(straight(p))
        def _():
            for k in range(zs):
                ag_y(p, k).wait_send()
            rs_y(p).wait_send()

        @pl.when(swapped(p))
        def _():
            column_sent(other_y)
            ag_y(p, z).wait_send()
            rs_y_one(p).wait_send()


def fused(position, coil_maps, kspace_data, sample_mask):
    rows, phases, slices, width = position.shape
    total = coil_maps.shape[1]
    zs = total // rows // YS
    side = zs * rows
    lanes = slices * width
    order = np.arange(total).reshape(zs, YS, rows).transpose(1, 0, 2).reshape(-1)
    row_real, row_imag = row_tables(total)
    rf = np.concatenate([row_real[:, order], row_imag[:, order]], 1)
    rb = np.concatenate([row_real[order], row_imag[order]], 1)
    forward, backward = wide_tables(width // 2)
    half = width // 2
    wf = np.concatenate([forward, -forward[:, half:], forward[:, :half]], 1)
    wb = np.concatenate([backward, backward[:, half:], backward[:, :half]], 1)


    vmem = pltpu.VMEM
    bf16, f32 = jnp.bfloat16, jnp.float32
    dma = pltpu.SemaphoreType.DMA
    return pl.pallas_call(
        functools.partial(kernel, zs, phases, rows, width),
        out_shape=jax.ShapeDtypeStruct(position.shape, f32),
        in_specs=[pl.BlockSpec(memory_space=pl.ANY if i == 2 else vmem) for i in range(8)],
        out_specs=pl.BlockSpec(memory_space=vmem),
        scratch_shapes=[
            vmem((phases, total, slices, width), bf16),
            vmem((2, phases, 1, lanes), f32),
            vmem((total, phases), f32),
            vmem((phases, rows, lanes), bf16),
            vmem((phases, YS, zs, rows, lanes), bf16),
            vmem((phases + 2, rows, lanes), f32),
            vmem((2, phases, 1, lanes), f32),
            vmem((total, lanes), f32),
            vmem((total, lanes), f32),
            vmem((2 * total, lanes), bf16),
            vmem((2 * total, lanes), bf16),
            vmem((phases, side, lanes), bf16),
            vmem((phases, side, lanes), bf16),
            vmem((phases, YS, side, lanes), f32),
            vmem((phases, rows, lanes), f32),
            vmem((phases, YS, zs, rows, lanes), bf16),
            vmem((phases, YS, 2, rows, lanes), bf16),
            vmem((phases, YS, 2, rows, lanes), bf16),
            dma((phases, YS, 4)), dma((phases, YS, zs)),
            dma((phases, zs)), dma((phases, zs)),
            dma((phases,)), dma((phases,)),
            dma((phases, YS, 3)), dma((phases, YS, 2)),
            dma((phases, YS)), dma((phases, YS)),
            dma((2,)), dma((2,)), dma((2,)), dma((2,)), dma((phases,)),
        ],
        compiler_params=pltpu.CompilerParams(
            collective_id=0, has_side_effects=True, vmem_limit_bytes=56 << 20
        ),
    )(position, coil_maps[0], kspace_data[0], sample_mask.T, jnp.asarray(rf), jnp.asarray(rb), jnp.asarray(wf), jnp.asarray(wb))


def with_halo(block, sides, width):
    for axis, dim in sides:
        count = lax.axis_size(axis)
        forward = [(i, i + 1) for i in range(count - 1)]
        forward.append((count - 1, 0))
        backward = [(target, source) for source, target in forward]
        low = lax.ppermute(
            lax.slice_in_dim(block, block.shape[dim] - width, None, axis=dim), axis, forward
        )
        high = lax.ppermute(lax.slice_in_dim(block, 0, width, axis=dim), axis, backward)
        block = jnp.concatenate([low, block, high], axis=dim)
    return block


def complex_times(factor, values, conjugate):
    width = values.shape[-1] // 2
    factor_real = factor[..., :width]
    factor_imag = factor[..., width:]
    if conjugate:
        factor_imag = -factor_imag
    value_real = values[..., :width]
    value_imag = values[..., width:]
    out_real = factor_real * value_real - factor_imag * value_imag
    out_imag = factor_real * value_imag + factor_imag * value_real
    return jnp.concatenate([out_real, out_imag], -1)


def rows_apply(table_real, table_imag, values, adjoint):
    width = values.shape[-1] // 2
    real_part = jnp.einsum("kn,npsd->kpsd", table_real, values, preferred_element_type=jnp.float32)
    imag_part = jnp.einsum("kn,npsd->kpsd", table_imag, values, preferred_element_type=jnp.float32)
    if adjoint:
        out_real = real_part[..., :width] + imag_part[..., width:]
        out_imag = real_part[..., width:] - imag_part[..., :width]
    else:
        out_real = real_part[..., :width] - imag_part[..., width:]
        out_imag = real_part[..., width:] + imag_part[..., :width]
    return jnp.concatenate([out_real, out_imag], -1)


def general(position, coil_maps, kspace_data, sample_mask):
    rows_total = coil_maps.shape[1]
    width = position.shape[3] // 2
    row_real, row_imag = (jnp.asarray(t) for t in row_tables(rows_total))
    forward_wide, backward_wide = (jnp.asarray(t) for t in wide_tables(width))
    coil_data = kspace_data[0]
    sample_weight = sample_mask.astype(jnp.float32)[:, :, None, None]
    position_low = position.astype(jnp.bfloat16)
    map_rows = coil_maps[0].astype(jnp.float32)[:, None]
    image = lax.all_gather(position_low, "coil", axis=0, tiled=True)
    lifted = complex_times(map_rows, image.astype(jnp.float32), False).astype(jnp.bfloat16)
    spread = jnp.einsum(
        "npsc,cd->npsd", lifted, forward_wide, preferred_element_type=jnp.float32
    ).astype(jnp.bfloat16)
    kspace = rows_apply(row_real, row_imag, spread, False)
    residual = (sample_weight * (kspace - coil_data.astype(jnp.float32))).astype(jnp.bfloat16)
    back_rows = rows_apply(row_real, row_imag, residual, True).astype(jnp.bfloat16)
    back = jnp.einsum("npsc,cd->npsd", back_rows, backward_wide, preferred_element_type=jnp.float32)
    likelihood = lax.psum_scatter(
        complex_times(map_rows, back, True), "coil", scatter_dimension=0, tiled=True
    )
    padded = with_halo(position, (("coil", 0), ("phase", 1)), 1)
    phase_part = 2.0 * position - padded[1:-1, :-2] - padded[1:-1, 2:]
    row_part = 2.0 * position - padded[:-2, 1:-1] - padded[2:, 1:-1]
    return 0.6 * likelihood + 0.5 * phase_part + 0.3 * row_part


def local(position, coil_maps, kspace_data, sample_mask):
    rows = position.shape[0]
    coils = lax.axis_size("coil")
    if coils == 8 and rows % 16 == 0 and position.shape[3] % 128 == 0:
        return fused(position, coil_maps, kspace_data, sample_mask)
    return general(position, coil_maps, kspace_data, sample_mask)


def solution(mesh):
    in_specs = (
        P("coil", "phase", "particle", None),
        P("coil", None, "particle", None),
        P("coil", None, "phase", "particle", None),
        P(None, "phase"),
    )
    out_specs = P("coil", "phase", "particle", None)
    return jax.shard_map(local, mesh=mesh, in_specs=in_specs, out_specs=out_specs, check_vma=False)
```
